512 devices in a mesh: elem: 64 (over z, y), mode: 8 (over x, core).
Axes of the slice: x: 4, y: 8, z: 8, core: 2. Of those that a mesh axis runs over, the one named last changes fastest.
Arguments:
- levels_rhs: float32 [128, 262144], P(None, ('elem', 'mode')), may hold values from -6 to 6
- to_modes: float32 [128, 128], replicated, may hold values from -0.5 to 0.5
- from_modes: float32 [128, 128], replicated, may hold values from -0.5 to 0.5
- helmholtz: float32 [128], replicated, may hold values from 0.5 to 50
- local_inverse: float32 [16, 16], replicated
- neighbor_ids: int32 [8, 16384], P(None, 'elem'), may hold values from 0 to 511, as said below
- neighbor_count: int32 [16384], P('elem'), may hold values from 7 to 8
- orientation: int32 [8, 16384], P(None, 'elem'), may hold values from 0 to 7
Outputs:
- levels_out: float32 [128, 262144], P(None, ('elem', 'mode'))
The draws below stay inside these ranges and needn't reach their ends.
Inputs may be any that keep to these rules, and one draw needn't show every extreme that they name: `neighbor_ids`: neighbour ids of an element of local index i in its elem block lie within i to i + 256.
All inputs are finite; a program needn't handle non-finite values.
Results may differ from the reference program's by a relative error of at most 0.0001.
Values sent between devices are 32-bit elements; how exact they have to be, the bound alone decides.
No kernel may reach another device: no remote copies, remote signals or barrier semaphores. Data moves between devices by JAX's collectives and lax.ppermute only.
A program may use at most 64 MiB of HBM per device.

```python
import math
import jax
import jax.numpy as jnp
from jax import lax

LEV = 128
NPTS = 16
NBR = 8
ELEM_BLOCK = 256
HALO = 128
NELEM = 16384
N_MODE = 8


def draw_local_inverse(key, part):
    noise = 0.15 * jax.random.normal(key, (NPTS, NPTS), jnp.float32)
    return jnp.eye(NPTS, dtype=jnp.float32) + noise


def draw_neighbor_ids(key, part):
    offsets = jax.random.randint(jax.random.fold_in(key, 11), (NBR, NELEM), -HALO, HALO + 1)
    local = (jnp.arange(NELEM, dtype=jnp.int32) % ELEM_BLOCK)[None, :]
    ids = local + HALO + offsets
    ids = ids.at[0, 0].set(0)
    ids = ids.at[0, NELEM - 1].set(ELEM_BLOCK + 2 * HALO - 1)
    return ids.astype(jnp.int32)


def draw_neighbor_count(key, part):
    corner = jax.random.randint(jax.random.fold_in(key, 23), (NELEM,), 0, 16)
    count = jnp.where(corner == 0, 7, 8).astype(jnp.int32)
    count = count.at[0].set(7)
    count = count.at[1].set(8)
    return count


def plant(array, own_key, low, high):
    spot = [jax.random.randint(jax.random.fold_in(own_key, axis), (), 0, length) for axis, length in enumerate(array.shape)]
    longest = array.shape.index(max(array.shape))
    next_to = spot[:longest] + [(spot[longest] + 1) % array.shape[longest]] + spot[longest + 1:]
    return array.at[tuple(spot)].set(low).at[tuple(next_to)].set(high)


def steps_of(stream_key, dims, cuts, least, high):
    def one(dim, parts):
        draws = jax.random.uniform(jax.random.fold_in(jax.random.fold_in(stream_key, 6), dim), (parts,), jnp.float32, least / len(cuts), high / len(cuts))
        return jnp.repeat(jnp.exp(draws), dims[dim] // parts).reshape((-1,) + (1,) * (len(dims) - dim - 1))

    factor_of = one(*cuts[0])
    for cut in cuts[1:]:
        factor_of = factor_of * one(*cut)
    return factor_of


def gaussian(stream_key, shape, scale, reach, cuts=(), kind=jnp.bfloat16):
    values = jax.random.normal(stream_key, shape, jnp.float32) * scale
    if len(cuts) > 0:
        values = steps_of(stream_key, shape, cuts, -0.22, 0.18) * values
    return jnp.clip(values, min=-reach, max=reach).astype(kind)


def setup_inputs(seed: int = 0) -> dict:
    key_list = jax.random.split(jax.random.key(seed), 9)
    return {
        "levels_rhs": gaussian(key_list[0], (LEV, NELEM * NPTS), 1.0, 6.0, ((1, 512),), jnp.float32),
        "to_modes": gaussian(key_list[1], (LEV, LEV), LEV ** -0.5, 0.5, (), jnp.float32),
        "from_modes": gaussian(key_list[2], (LEV, LEV), LEV ** -0.5, 0.5, (), jnp.float32),
        "helmholtz": jnp.clip(jnp.exp(jax.random.uniform(key_list[3], (LEV,), jnp.float32, math.log(0.5), math.log(50.0))), 0.5, 50.0),
        "local_inverse": draw_local_inverse(jax.random.fold_in(key_list[8], 71), 0),
        "neighbor_ids": draw_neighbor_ids(jax.random.fold_in(key_list[8], 71), 0),
        "neighbor_count": draw_neighbor_count(jax.random.fold_in(key_list[8], 71), 0),
        "orientation": plant(jax.random.randint(key_list[7], (NBR, NELEM), 0, 8), jax.random.fold_in(key_list[7], 1), 0, 7).astype(jnp.int32),
    }


def oriented_points(code, points):
    row = points // 4
    col = points % 4
    swap = code % 2
    flip_row = (code // 2) % 2
    flip_col = (code // 4) % 2
    row_two = jnp.where(swap == 1, col, row)
    col_two = jnp.where(swap == 1, row, col)
    row_three = jnp.where(flip_row == 1, 3 - row_two, row_two)
    col_three = jnp.where(flip_col == 1, 3 - col_two, col_two)
    return (row_three * 4 + col_three).astype(jnp.int32)


def schwarz_sweep(u_own, u_ext, rhs_part, index, orientation, count, coeff, local_inverse):
    modes = u_ext.shape[0]
    width = u_ext.shape[2]
    elems = index.shape[1]
    flat = u_ext.reshape(modes, 16 * width)
    points = jnp.arange(16, dtype=jnp.int32)[:, None]
    total = jnp.zeros((modes, 16, elems), jnp.float32)
    for slot in range(8):
        perm = oriented_points(orientation[slot][None, :], points)
        where_at = perm * width + index[slot][None, :]
        picked = jnp.take(flat, where_at.reshape(-1), axis=1).reshape(modes, 16, elems)
        used = (slot < count)[None, None, :]
        total = total + jnp.where(used, picked, 0.0)
    scale = coeff[:, None, None]
    countf = count.astype(jnp.float32)[None, None, :]
    resid = rhs_part - (1.0 + scale) * u_own + scale * total / countf
    fix = jnp.einsum("pq,mqe->mpe", local_inverse, resid, precision=lax.Precision.HIGHEST)
    return u_own + fix / (1.0 + scale)


def reference(levels_rhs, to_modes, from_modes, helmholtz, local_inverse, neighbor_ids, neighbor_count, orientation):
    levels_cube = jnp.transpose(levels_rhs.reshape(LEV, NELEM, 16), (0, 2, 1))
    rhs_modes = jnp.einsum("ml,lpe->mpe", to_modes, levels_cube, precision=lax.Precision.HIGHEST)
    elem_iota = jnp.arange(NELEM, dtype=jnp.int32)
    start = (elem_iota // ELEM_BLOCK) * ELEM_BLOCK
    global_ids = (start[None, :] + neighbor_ids - HALO) % NELEM
    global_ids = global_ids.astype(jnp.int32)
    group_modes = LEV // N_MODE

    def per_group(items):
        rhs_group, coeff_group = items
        u_now = rhs_group / (1.0 + coeff_group[:, None, None])
        for sweep_index in range(2):
            u_now = schwarz_sweep(u_now, u_now, rhs_group, global_ids, orientation, neighbor_count, coeff_group, local_inverse)
        return u_now

    grouped = rhs_modes.reshape(N_MODE, group_modes, 16, NELEM)
    coeffs = helmholtz.reshape(N_MODE, group_modes)
    u_final = lax.map(per_group, (grouped, coeffs)).reshape(LEV, 16, NELEM)
    result = jnp.einsum("lm,mpe->lpe", from_modes, u_final, precision=lax.Precision.HIGHEST)
    return jnp.transpose(result, (0, 2, 1)).reshape(LEV, NELEM * 16)
```

```python
import functools

import jax
import jax.numpy as jnp
from jax import lax
from jax.experimental import pallas as pl
from jax.experimental.pallas import tpu as pltpu
from jax.sharding import PartitionSpec as P


def split(x):
    high = x.astype(jnp.bfloat16)
    return high, (x - high.astype(jnp.float32)).astype(jnp.bfloat16)


def dot(a, b):
    return jnp.dot(a, b, preferred_element_type=jnp.float32)


def dot3(a, b):
    ah, al = split(a)
    bh, bl = split(b)
    return dot(ah, bh) + (dot(ah, bl) + dot(al, bh))


def to_modes_kernel(rhs_ref, modes_ref, scale_ref, out_ref):
    row = lax.broadcasted_iota(jnp.int32, (512, 512), 0)
    col = lax.broadcasted_iota(jnp.int32, (1, 512), 1)
    perm = (row == (col % 32) * 16 + col // 32).astype(jnp.float32).astype(jnp.bfloat16)
    high, low = split(rhs_ref[...])
    high = dot(high, perm).astype(jnp.bfloat16)
    low = dot(low, perm).astype(jnp.bfloat16)
    mh, ml = split(modes_ref[...])
    start = (dot(mh, high) + (dot(mh, low) + dot(ml, high))) * scale_ref[...]
    for group in range(8):
        for quad in range(4):
            part = start[16 * group : 16 * group + 16, 128 * quad : 128 * quad + 128]
            for copy in range(2):
                out_ref[8 * copy + group, 16 * quad : 16 * quad + 16, :] = part


def transpose_quads(parts):
    rows = parts[0].shape[0]
    where_at = lax.broadcasted_iota(jnp.int32, (rows, 128), 1) // 32
    outs = []
    for i in range(4):
        out = None
        for j in range(4):
            shift = (32 * (j - i)) % 128
            moved = parts[j] if shift == 0 else pltpu.roll(parts[j], shift, 1)
            out = moved if out is None else jnp.where(where_at == j, moved, out)
        outs.append(out)
    return outs


def half_table(tables, half, odd):
    even_at, odd_at = half + 2, 3 - half
    even_ref, odd_ref = tables[even_at // 2], tables[odd_at // 2]
    even_half, odd_half = even_at % 2, odd_at % 2
    even = even_ref[:, 128 * even_half : 128 * even_half + 128]
    other = odd_ref[:, 128 * odd_half : 128 * odd_half + 128]
    even_ids, other_ids = even[0:8], other[0:8]
    step = jnp.where(odd, 1 + odd_half - (other_ids >> 7), (even_ids >> 7) - 1 - even_half)
    both = jnp.where(odd, other, even)
    lane = both[0:8] & 127
    code = both[8:16]
    count = both[16:17]
    slot = lax.broadcasted_iota(jnp.int32, (8, 128), 0)
    step = jnp.where(slot < count, step, 9)
    return lane, step, code, 1.0 / count.astype(jnp.float32)


def gathered(src_ref, sources, table, row):
    lane, step, code, inv = table
    total = [jnp.zeros((8, 128), jnp.float32) for _ in range(16)]
    for k in range(8):
        spread = lambda x: jnp.broadcast_to(x[k : k + 1], (8, 128))
        lane_k, step_k, code_k = spread(lane), spread(step), spread(code)
        swap = (code_k & 1) == 1
        flip_row = (code_k & 2) == 2
        flip_col = (code_k & 4) == 4
        at = [step_k == d for d in sources]
        picked = []
        for p in range(16):
            value = jnp.zeros((8, 128), jnp.float32)
            for is_d, d in zip(at, sources):
                block = src_ref[sources[d], pl.ds(16 * p + row, 8), :]
                value = jnp.where(is_d, jnp.take_along_axis(block, lane_k, axis=1), value)
            picked.append(value)
        rows = [jnp.where(flip_row, picked[4 * (3 - i) + j], picked[4 * i + j]) for i in range(4) for j in range(4)]
        cols = [jnp.where(flip_col, rows[4 * i + 3 - j], rows[4 * i + j]) for i in range(4) for j in range(4)]
        for i in range(4):
            for j in range(4):
                p = 4 * i + j
                value = cols[p] if i == j else jnp.where(swap, cols[4 * j + i], cols[p])
                total[p] = total[p] + value
    return [t * inv for t in total]


def sweep_kernel(odd_ref, x_ref, before_ref, own_ref, after_ref, weight_ref, inverse_ref, out_ref, u_ref, w_ref, s_ref):
    odd = odd_ref[0] == 1
    tables = (before_ref, own_ref, after_ref)
    for half in range(4):
        base = 4 * jnp.where(odd, 3 - half, half)
        for quad in range(4):
            parts = [x_ref[base + j, 16 * quad : 16 * quad + 16, :] for j in range(4)]
            for i, part in enumerate(transpose_quads(parts)):
                u_ref[half, 64 * quad + 16 * i : 64 * quad + 16 * i + 16, :] = part
    inverse = inverse_ref[...]
    for place, half in enumerate((-1, 0, 1, 2)):
        table = half_table(tables, half, odd)
        sources = {d: half + d for d in (-1, 0, 1) if 0 <= half + d <= 3}

        def first(m, carry, place=place, table=table, sources=sources):
            row = pl.multiple_of(8 * m, 8)
            weight = weight_ref[pl.ds(row, 8), :]
            for p, value in enumerate(gathered(u_ref, sources, table, row)):
                s_ref[pl.ds(16 * p + row, 8), 128 * place : 128 * place + 128] = weight * value
            return carry

        lax.fori_loop(0, 2, first, 0)
    fixed = dot3(inverse, s_ref[...])
    for place in range(4):
        w_ref[place] = fixed[:, 128 * place : 128 * place + 128]
    for place, half in enumerate((-2, -1, 0, 1)):
        table = half_table(tables, half, odd)
        sources = {d: half + d + 1 for d in (-1, 0, 1) if 0 <= half + d + 1 <= 3}

        def second(m, carry, place=place, half=half, table=table, sources=sources):
            row = pl.multiple_of(8 * m, 8)
            weight = weight_ref[pl.ds(row, 8), :]
            for p, value in enumerate(gathered(w_ref, sources, table, row)):
                value = weight * value
                if half >= -1:
                    value = value - w_ref[half + 1, pl.ds(16 * p + row, 8), :]
                s_ref[pl.ds(16 * p + row, 8), 128 * place : 128 * place + 128] = value
            return carry

        lax.fori_loop(0, 2, second, 0)
    fixed = dot3(inverse, s_ref[...])
    for place, half in enumerate((-2, -1, 0, 1)):
        base = 4 * jnp.where(odd, 3 - place, place)
        for quad in range(4):
            parts = []
            for i in range(4):
                rows = slice(64 * quad + 16 * i, 64 * quad + 16 * i + 16)
                value = fixed[rows, 128 * place : 128 * place + 128]
                if half >= -1:
                    value = value + 2.0 * w_ref[half + 1, rows, :]
                if half >= 0:
                    value = value + u_ref[half, rows, :]
                parts.append(value)
            for j, part in enumerate(transpose_quads(parts)):
                out_ref[base + j, 16 * quad : 16 * quad + 16, :] = part


def to_levels_kernel(parts_ref, levels_ref, out_ref, modes_ref):
    for group in range(8):
        for quad in range(4):
            rows = slice(16 * quad, 16 * quad + 16)
            modes_ref[16 * group : 16 * group + 16, 128 * quad : 128 * quad + 128] = (
                parts_ref[group, rows, :] + parts_ref[8 + group, rows, :]
            )
    high, low = split(dot3(levels_ref[...], modes_ref[...]))
    row = lax.broadcasted_iota(jnp.int32, (512, 512), 0)
    col = lax.broadcasted_iota(jnp.int32, (1, 512), 1)
    perm = (row == (col % 16) * 32 + col // 16).astype(jnp.float32).astype(jnp.bfloat16)
    out_ref[...] = dot(high, perm) + dot(low, perm)


def shapes(*dims):
    return jax.ShapeDtypeStruct(dims, jnp.float32)


def cost(flops, moved):
    return pl.CostEstimate(flops=flops, bytes_accessed=moved, transcendentals=0)


def body(blocks, levels_rhs, to_modes, from_modes, helmholtz, local_inverse, neighbor_ids, neighbor_count, orientation):
    axes = ("elem", "mode")
    parts = lax.axis_size("mode")
    source_pairs = [[(2 * k + i) * parts + j for i in range(2) for j in range(parts)] for k in range(blocks // 2)]
    target_pairs = [
        [((2 * k - 1 + i) % blocks) * parts + j for i in range(2) for j in range(parts)] for k in range(blocks // 2)
    ]
    forward = [(i, (i + 1) % blocks) for i in range(blocks)]
    backward = [(b, a) for a, b in forward]

    table = jnp.concatenate([neighbor_ids, orientation, neighbor_count[None]], axis=0)
    before = lax.ppermute(table, "elem", forward)
    after = lax.ppermute(table, "elem", backward)

    start = pl.pallas_call(
        to_modes_kernel,
        out_shape=shapes(16, 64, 128),
        cost_estimate=cost(2 * 128 * 512 * (512 + 128), 1 << 20),
        name="to_modes_chunks",
    )(levels_rhs, to_modes, 1.0 / (1.0 + helmholtz)[:, None])
    sources = lax.all_to_all(start, axes, 0, 0, axis_index_groups=source_pairs, tiled=True)

    coeff = lax.dynamic_slice_in_dim(helmholtz, lax.axis_index("mode") * 16, 16, 0)
    weight = jnp.broadcast_to((coeff / (1.0 + coeff))[:, None], (16, 128))
    inverse = jnp.kron(local_inverse, jnp.eye(16, dtype=jnp.float32))
    odd = jnp.broadcast_to(lax.axis_index("elem") % 2, (1,)).astype(jnp.int32)
    vmem = pl.BlockSpec(memory_space=pltpu.VMEM)
    targets = pl.pallas_call(
        sweep_kernel,
        out_shape=shapes(16, 64, 128),
        in_specs=[pl.BlockSpec(memory_space=pltpu.SMEM)] + [vmem] * 6,
        out_specs=vmem,
        scratch_shapes=[
            pltpu.VMEM((4, 256, 128), jnp.float32),
            pltpu.VMEM((4, 256, 128), jnp.float32),
            pltpu.VMEM((256, 512), jnp.float32),
        ],
        cost_estimate=cost(1 << 30, 2 << 20),
        name="two_sweeps",
    )(odd, sources, before, table, after, weight, inverse)
    whole = lax.all_to_all(targets, axes, 0, 0, axis_index_groups=target_pairs, tiled=True)
    return pl.pallas_call(
        to_levels_kernel,
        out_shape=shapes(128, 512),
        scratch_shapes=[pltpu.VMEM((128, 512), jnp.float32)],
        cost_estimate=cost(2 * 128 * 512 * (512 + 128), 1 << 20),
        name="to_levels",
    )(whole, from_modes)


def solution(mesh):
    in_specs = (
        P(None, ("elem", "mode")),
        P(),
        P(),
        P(),
        P(),
        P(None, "elem"),
        P("elem"),
        P(None, "elem"),
    )
    out_specs = P(None, ("elem", "mode"))
    return jax.shard_map(
        functools.partial(body, mesh.shape["elem"]), mesh=mesh, in_specs=in_specs, out_specs=out_specs, check_vma=False
    )
```

```python
import functools

import jax
import jax.numpy as jnp
from jax import lax
from jax.experimental import pallas as pl
from jax.experimental.pallas import tpu as pltpu
from jax.sharding import PartitionSpec as P


def split(x):
    high = x.astype(jnp.bfloat16)
    return high, (x - high.astype(jnp.float32)).astype(jnp.bfloat16)


def dot(a, b):
    return jnp.dot(a, b, preferred_element_type=jnp.float32)


def dot3(a, b):
    ah, al = split(a)
    bh, bl = split(b)
    return dot(ah, bh) + (dot(ah, bl) + dot(al, bh))


def column(row):
    count = row.shape[1]
    at = lax.broadcasted_iota(jnp.int32, (count, count), 0) == lax.broadcasted_iota(jnp.int32, (count, count), 1)
    return jnp.sum(jnp.where(at, row, 0.0), axis=1, keepdims=True)


def fetch(pairs, sems):
    copies = [pltpu.make_async_copy(src, dst, sems.at[i]) for i, (src, dst) in enumerate(pairs)]
    for copy in copies:
        copy.start()
    return copies


def to_modes_kernel(
    rhs_hbm, modes_hbm, helmholtz_hbm, ids_hbm, orientation_hbm, count_hbm,
    out_ref, table_ref, rhs_ref, modes_ref, helmholtz_ref, count_ref, sems,
):
    copies = fetch(
        (
            (rhs_hbm, rhs_ref),
            (modes_hbm, modes_ref),
            (helmholtz_hbm, helmholtz_ref),
            (ids_hbm, table_ref.at[0:8]),
            (orientation_hbm, table_ref.at[8:16]),
            (count_hbm, count_ref),
        ),
        sems,
    )
    row = lax.broadcasted_iota(jnp.int32, (512, 512), 0)
    col = lax.broadcasted_iota(jnp.int32, (1, 512), 1)
    perm = (row == (col % 32) * 16 + col // 32).astype(jnp.float32).astype(jnp.bfloat16)
    for copy in copies:
        copy.wait()
    table_ref[16:24] = jnp.broadcast_to(count_ref[...], (8, 256))
    high, low = split(rhs_ref[...])
    high = dot(high, perm).astype(jnp.bfloat16)
    low = dot(low, perm).astype(jnp.bfloat16)
    mh, ml = split(modes_ref[...] * column(1.0 / (1.0 + helmholtz_ref[...])))
    start = dot(mh, high) + (dot(mh, low) + dot(ml, high))
    for group in range(8):
        for quad in range(4):
            part = start[16 * group : 16 * group + 16, 128 * quad : 128 * quad + 128]
            for copy in range(2):
                out_ref[8 * copy + group, 16 * quad : 16 * quad + 16, :] = part


def transpose_quads(parts):
    rows = parts[0].shape[0]
    where_at = lax.broadcasted_iota(jnp.int32, (rows, 128), 1) // 32
    outs = []
    for i in range(4):
        out = None
        for j in range(4):
            shift = (32 * (j - i)) % 128
            moved = parts[j] if shift == 0 else pltpu.roll(parts[j], shift, 1)
            out = moved if out is None else jnp.where(where_at == j, moved, out)
        outs.append(out)
    return outs


REACH = {-2: (1,), -1: (0, 1), 0: (-1, 0, 1), 1: (-1, 0, 1), 2: (-1, 0, 1)}
OWN = {0: 0, 1: 3}
OTHER = {-2: 0, -1: 1, 2: 3}


def half_table(table_ref, half, odd):
    even_half, odd_half = half % 2, (half + 1) % 2
    even = table_ref[:, 128 * even_half : 128 * even_half + 128]
    other = table_ref[:, 128 * odd_half : 128 * odd_half + 128]
    step = jnp.where(odd, 1 + odd_half - (other[0:8] >> 7), (even[0:8] >> 7) - 1 - even_half)
    both = jnp.where(odd, other, even)
    count = both[16:24]
    slot = lax.broadcasted_iota(jnp.int32, (8, 128), 0)
    return both[0:8] & 127, jnp.where(slot < count, step, 9), both[8:16], 1.0 / count[0:1].astype(jnp.float32)


def write_picks(table_ref, half, odd, pick_ref, at):
    lane, step, code, inv = half_table(table_ref, half, odd)
    source = lax.broadcasted_iota(jnp.int32, (128, 128), 0)
    for i, d in enumerate(REACH[half]):
        wanted = jnp.where(step == d, lane, -1)
        for k in range(8):
            pick = (source == wanted[k : k + 1]).astype(jnp.float32).astype(jnp.bfloat16)
            pick_ref[k // 2, at + i, :, 128 * (k % 2) : 128 * (k % 2) + 128] = pick
    return code, inv


def tables_kernel(
    place_ref, own_ref, helmholtz_hbm, inverse_hbm,
    pick_ref, code_ref, weight_ref, inv_ref, high_ref, low_ref, again_ref, helmholtz_ref, inverse_ref, sems,
):
    again_ref[...] = own_ref[...]
    copies = fetch(((helmholtz_hbm, helmholtz_ref), (inverse_hbm, inverse_ref)), sems)
    odd = place_ref[0] == 1
    for half in (0, 1):
        code, inv = write_picks(own_ref, half, odd, pick_ref, 3 * half)
        code_ref[half] = code
        inv_ref[half] = jnp.broadcast_to(inv, (8, 128))
    for copy in copies:
        copy.wait()
    rows = lax.broadcasted_iota(jnp.int32, (16, 128), 0)
    lanes = lax.broadcasted_iota(jnp.int32, (16, 128), 1)
    coeff = jnp.sum(jnp.where(lanes == rows + 16 * place_ref[1], helmholtz_ref[...], 0.0), axis=1, keepdims=True)
    weight_ref[...] = jnp.broadcast_to(coeff / (1.0 + coeff), (16, 128))
    big = lax.broadcasted_iota(jnp.int32, (256, 16), 0) // 16 == lax.broadcasted_iota(jnp.int32, (256, 16), 1)
    rise = big.astype(jnp.float32).astype(jnp.bfloat16)
    wide = lax.broadcasted_iota(jnp.int32, (16, 256), 1) // 16 == lax.broadcasted_iota(jnp.int32, (16, 256), 0)
    spread = wide.astype(jnp.float32).astype(jnp.bfloat16)
    same = (
        lax.broadcasted_iota(jnp.int32, (256, 256), 0) % 16 == lax.broadcasted_iota(jnp.int32, (256, 256), 1) % 16
    )
    for ref, part in zip((high_ref, low_ref), split(inverse_ref[...])):
        ref[...] = jnp.where(same, dot(dot(rise, part).astype(jnp.bfloat16), spread), 0.0).astype(jnp.bfloat16)


def neighbor_sum(split_ref, first, count, pick_ref, at, code):
    total = [[None] * 16 for _ in range(2)]
    lhs = split_ref[:, 256 * first : 256 * (first + count)]
    for pair in range(4):
        rhs = jnp.concatenate([pick_ref[pair, at + c // 2] for c in range(2 * count)], axis=0)
        found = dot(lhs, rhs)
        for side in range(2):
            code_k = jnp.broadcast_to(code[2 * pair + side : 2 * pair + side + 1], (8, 128))
            swap = (code_k & 1) == 1
            flip_row = (code_k & 2) == 2
            flip_col = (code_k & 4) == 4
            for m in range(2):
                x = [found[16 * p + 8 * m : 16 * p + 8 * m + 8, 128 * side : 128 * side + 128] for p in range(16)]
                x = [jnp.where(flip_row, x[4 * (3 - i) + j], x[4 * i + j]) for i in range(4) for j in range(4)]
                x = [jnp.where(flip_col, x[4 * i + 3 - j], x[4 * i + j]) for i in range(4) for j in range(4)]
                x = [x[5 * i] if i == j else jnp.where(swap, x[4 * j + i], x[4 * i + j]) for i in range(4) for j in range(4)]
                total[m] = [v if t is None else t + v for t, v in zip(total[m], x)]
    return total


def fix(high_ref, low_ref, x):
    xh, xl = split(x)
    return dot(high_ref[...], xh) + (dot(high_ref[...], xl) + dot(low_ref[...], xh))


def sweep_kernel(
    place_ref, x_ref, source_table_ref, target_table_ref, pick_ref, code_ref, weight_ref, inv_ref, high_ref, low_ref,
    out_ref, u_ref, w_ref, us_ref, ws_ref, s_ref, other_ref,
):
    odd = place_ref[0] == 1
    known = {half: (code_ref[half], inv_ref[half]) for half in OWN}
    for half in OTHER:
        table_ref = source_table_ref if half == 2 else target_table_ref
        known[half] = write_picks(table_ref, half, odd, other_ref, OTHER[half])
    for half in range(4):
        base = 4 * jnp.where(odd, 3 - half, half)
        for quad in range(4):
            parts = [x_ref[base + j, 16 * quad : 16 * quad + 16, :] for j in range(4)]
            for i, part in enumerate(transpose_quads(parts)):
                rows = slice(64 * quad + 16 * i, 64 * quad + 16 * i + 16)
                u_ref[half, rows, :] = part
                high, low = split(part)
                us_ref[rows, 256 * half : 256 * half + 128] = high
                us_ref[rows, 256 * half + 128 : 256 * half + 256] = low
    for place, half in enumerate((-1, 0, 1, 2)):
        steps = [d for d in REACH[half] if 0 <= half + d <= 3]
        picks, at = (pick_ref, OWN[half]) if half in OWN else (other_ref, OTHER[half])
        code, inv = known[half]
        total = neighbor_sum(us_ref, half + steps[0], len(steps), picks, at + REACH[half].index(steps[0]), code)
        for m in range(2):
            weight = weight_ref[8 * m : 8 * m + 8, :] * inv
            for p in range(16):
                s_ref[16 * p + 8 * m : 16 * p + 8 * m + 8, 128 * place : 128 * place + 128] = weight * total[m][p]
    fixed = fix(high_ref, low_ref, s_ref[...])
    for place in range(4):
        part = fixed[:, 128 * place : 128 * place + 128]
        w_ref[place] = part
        high, low = split(part)
        ws_ref[:, 256 * place : 256 * place + 128] = high
        ws_ref[:, 256 * place + 128 : 256 * place + 256] = low
    for place, half in enumerate((-2, -1, 0, 1)):
        steps = [d for d in REACH[half] if -1 <= half + d <= 2]
        picks, at = (pick_ref, OWN[half]) if half in OWN else (other_ref, OTHER[half])
        code, inv = known[half]
        total = neighbor_sum(ws_ref, half + steps[0] + 1, len(steps), picks, at + REACH[half].index(steps[0]), code)
        for m in range(2):
            weight = weight_ref[8 * m : 8 * m + 8, :] * inv
            for p in range(16):
                rows = slice(16 * p + 8 * m, 16 * p + 8 * m + 8)
                value = weight * total[m][p]
                if half >= -1:
                    value = value - w_ref[half + 1, rows, :]
                s_ref[rows, 128 * place : 128 * place + 128] = value
    fixed = fix(high_ref, low_ref, s_ref[...])
    for place, half in enumerate((-2, -1, 0, 1)):
        base = 4 * jnp.where(odd, 3 - place, place)
        for quad in range(4):
            parts = []
            for i in range(4):
                rows = slice(64 * quad + 16 * i, 64 * quad + 16 * i + 16)
                value = fixed[rows, 128 * place : 128 * place + 128]
                if half >= -1:
                    value = value + 2.0 * w_ref[half + 1, rows, :]
                if half >= 0:
                    value = value + u_ref[half, rows, :]
                parts.append(value)
            for j, part in enumerate(transpose_quads(parts)):
                out_ref[base + j, 16 * quad : 16 * quad + 16, :] = part


def to_levels_kernel(parts_ref, levels_ref, out_ref, modes_ref):
    for group in range(8):
        for quad in range(4):
            rows = slice(16 * quad, 16 * quad + 16)
            modes_ref[16 * group : 16 * group + 16, 128 * quad : 128 * quad + 128] = (
                parts_ref[group, rows, :] + parts_ref[8 + group, rows, :]
            )
    high, low = split(dot3(levels_ref[...], modes_ref[...]))
    row = lax.broadcasted_iota(jnp.int32, (512, 512), 0)
    col = lax.broadcasted_iota(jnp.int32, (1, 512), 1)
    perm = (row == (col % 16) * 32 + col // 16).astype(jnp.float32).astype(jnp.bfloat16)
    out_ref[...] = dot(high, perm) + dot(low, perm)


def cost(flops, moved):
    return pl.CostEstimate(flops=flops, bytes_accessed=moved, transcendentals=0)


def near(x):
    return pltpu.with_memory_space_constraint(x, pltpu.VMEM)


def far(x):
    return pltpu.with_memory_space_constraint(x, pltpu.HBM)


VMEM = pl.BlockSpec(memory_space=pltpu.VMEM)
SMEM = pl.BlockSpec(memory_space=pltpu.SMEM)
HBM = pl.BlockSpec(memory_space=pltpu.HBM)
LIMIT = pltpu.CompilerParams(vmem_limit_bytes=20 << 20)


def body(blocks, levels_rhs, to_modes, from_modes, helmholtz, local_inverse, neighbor_ids, neighbor_count, orientation):
    axes = ("elem", "mode")
    parts = lax.axis_size("mode")
    source_pairs = [[(2 * k + i) * parts + j for i in range(2) for j in range(parts)] for k in range(blocks // 2)]
    target_pairs = [
        [((2 * k - 1 + i) % blocks) * parts + j for i in range(2) for j in range(parts)] for k in range(blocks // 2)
    ]
    source_swap = [(b, b ^ 1) for b in range(blocks)]
    target_swap = [(b, (((b + 1) ^ 1) - 1) % blocks) for b in range(blocks)]
    helmholtz = helmholtz[None]
    place = jnp.stack([lax.axis_index("elem") % 2, lax.axis_index("mode")]).astype(jnp.int32)

    start, own = pl.pallas_call(
        to_modes_kernel,
        out_shape=(pltpu.VMEM((16, 64, 128), jnp.float32), pltpu.VMEM((24, 256), jnp.int32)),
        in_specs=[HBM] * 6,
        out_specs=(VMEM, VMEM),
        scratch_shapes=[
            pltpu.VMEM((128, 512), jnp.float32),
            pltpu.VMEM((128, 128), jnp.float32),
            pltpu.VMEM((1, 128), jnp.float32),
            pltpu.VMEM((1, 256), jnp.int32),
            pltpu.SemaphoreType.DMA((6,)),
        ],
        compiler_params=LIMIT,
        cost_estimate=cost(2 * 128 * 512 * (512 + 128), 1 << 20),
        name="to_modes_chunks",
    )(*[far(x) for x in (levels_rhs, to_modes, helmholtz, neighbor_ids, orientation, neighbor_count[None])])
    sources = lax.all_to_all(start, axes, 0, 0, axis_index_groups=source_pairs, tiled=True)
    source_table = lax.ppermute(own, "elem", source_swap)
    *parts_of_tables, again = pl.pallas_call(
        tables_kernel,
        out_shape=(
            pltpu.VMEM((4, 6, 128, 256), jnp.bfloat16),
            pltpu.VMEM((2, 8, 128), jnp.int32),
            pltpu.VMEM((16, 128), jnp.float32),
            pltpu.VMEM((2, 8, 128), jnp.float32),
            pltpu.VMEM((256, 256), jnp.bfloat16),
            pltpu.VMEM((256, 256), jnp.bfloat16),
            pltpu.VMEM((24, 256), jnp.int32),
        ),
        in_specs=[SMEM, VMEM, HBM, HBM],
        out_specs=(VMEM,) * 7,
        scratch_shapes=[
            pltpu.VMEM((1, 128), jnp.float32),
            pltpu.VMEM((16, 16), jnp.float32),
            pltpu.SemaphoreType.DMA((2,)),
        ],
        compiler_params=LIMIT,
        cost_estimate=cost(1 << 28, 2 << 20),
        name="own_tables",
    )(place, near(own), far(helmholtz), far(local_inverse))
    target_table = lax.ppermute(again, "elem", target_swap)
    targets = pl.pallas_call(
        sweep_kernel,
        out_shape=pltpu.VMEM((16, 64, 128), jnp.float32),
        in_specs=[SMEM] + [VMEM] * 9,
        out_specs=VMEM,
        scratch_shapes=[
            pltpu.VMEM((4, 256, 128), jnp.float32),
            pltpu.VMEM((4, 256, 128), jnp.float32),
            pltpu.VMEM((256, 1024), jnp.bfloat16),
            pltpu.VMEM((256, 1024), jnp.bfloat16),
            pltpu.VMEM((256, 512), jnp.float32),
            pltpu.VMEM((4, 6, 128, 256), jnp.bfloat16),
        ],
        compiler_params=LIMIT,
        cost_estimate=cost(4 << 30, 8 << 20),
        name="two_sweeps",
    )(place, near(sources), near(source_table), near(target_table), *[near(part) for part in parts_of_tables])
    whole = lax.all_to_all(targets, axes, 0, 0, axis_index_groups=target_pairs, tiled=True)
    return pl.pallas_call(
        to_levels_kernel,
        out_shape=jax.ShapeDtypeStruct((128, 512), jnp.float32),
        in_specs=[VMEM] * 2,
        out_specs=VMEM,
        scratch_shapes=[pltpu.VMEM((128, 512), jnp.float32)],
        compiler_params=LIMIT,
        cost_estimate=cost(2 * 128 * 512 * (512 + 128), 1 << 20),
        name="to_levels",
    )(near(whole), from_modes)


def solution(mesh):
    in_specs = (
        P(None, ("elem", "mode")),
        P(),
        P(),
        P(),
        P(),
        P(None, "elem"),
        P("elem"),
        P(None, "elem"),
    )
    out_specs = P(None, ("elem", "mode"))
    return jax.shard_map(
        functools.partial(body, mesh.shape["elem"]), mesh=mesh, in_specs=in_specs, out_specs=out_specs, check_vma=False
    )
```

```python
import functools

import jax
import jax.numpy as jnp
from jax import lax
from jax.experimental import pallas as pl
from jax.experimental.pallas import tpu as pltpu
from jax.sharding import PartitionSpec as P


def split(x):
    high = x.astype(jnp.bfloat16)
    return high, (x - high.astype(jnp.float32)).astype(jnp.bfloat16)


def dot(a, b):
    return jnp.dot(a, b, preferred_element_type=jnp.float32)


def dot3(a, b):
    ah, al = split(a)
    bh, bl = split(b)
    return dot(ah, bh) + (dot(ah, bl) + dot(al, bh))


def column(row):
    count = row.shape[1]
    at = lax.broadcasted_iota(jnp.int32, (count, count), 0) == lax.broadcasted_iota(jnp.int32, (count, count), 1)
    return jnp.sum(jnp.where(at, row, 0.0), axis=1, keepdims=True)


def fetch(pairs, sems):
    copies = [pltpu.make_async_copy(src, dst, sems.at[i]) for i, (src, dst) in enumerate(pairs)]
    for copy in copies:
        copy.start()
    return copies


def to_modes_kernel(
    rhs_hbm, modes_hbm, helmholtz_hbm, ids_hbm, orientation_hbm, count_hbm,
    out_ref, table_ref, rhs_ref, modes_ref, helmholtz_ref, count_ref, sems,
):
    copies = fetch(
        (
            (rhs_hbm, rhs_ref),
            (modes_hbm, modes_ref),
            (helmholtz_hbm, helmholtz_ref),
            (ids_hbm, table_ref.at[0:8]),
            (orientation_hbm, table_ref.at[8:16]),
            (count_hbm, count_ref),
        ),
        sems,
    )
    row = lax.broadcasted_iota(jnp.int32, (512, 512), 0)
    col = lax.broadcasted_iota(jnp.int32, (1, 512), 1)
    perm = (row == (col % 32) * 16 + col // 32).astype(jnp.float32).astype(jnp.bfloat16)
    for copy in copies:
        copy.wait()
    table_ref[16:24] = jnp.broadcast_to(count_ref[...], (8, 256))
    high, low = split(rhs_ref[...])
    high = dot(high, perm).astype(jnp.bfloat16)
    low = dot(low, perm).astype(jnp.bfloat16)
    mh, ml = split(modes_ref[...] * column(1.0 / (1.0 + helmholtz_ref[...])))
    start = dot(mh, high) + (dot(mh, low) + dot(ml, high))
    for group in range(8):
        for quad in range(4):
            part = start[16 * group : 16 * group + 16, 128 * quad : 128 * quad + 128]
            for copy in range(2):
                out_ref[8 * copy + group, 16 * quad : 16 * quad + 16, :] = part


def transpose_quads(parts):
    rows = parts[0].shape[0]
    where_at = lax.broadcasted_iota(jnp.int32, (rows, 128), 1) // 32
    outs = []
    for i in range(4):
        out = None
        for j in range(4):
            shift = (32 * (j - i)) % 128
            moved = parts[j] if shift == 0 else pltpu.roll(parts[j], shift, 1)
            out = moved if out is None else jnp.where(where_at == j, moved, out)
        outs.append(out)
    return outs


REACH = {-2: (1,), -1: (0, 1), 0: (-1, 0, 1), 1: (-1, 0, 1), 2: (-1, 0, 1)}
OWN = {0: 0, 1: 3}
OTHER = {-2: 0, -1: 1, 2: 3}


def half_table(table_ref, half, odd):
    even_half, odd_half = half % 2, (half + 1) % 2
    even = table_ref[:, 128 * even_half : 128 * even_half + 128]
    other = table_ref[:, 128 * odd_half : 128 * odd_half + 128]
    step = jnp.where(odd, 1 + odd_half - (other[0:8] >> 7), (even[0:8] >> 7) - 1 - even_half)
    both = jnp.where(odd, other, even)
    count = both[16:24]
    slot = lax.broadcasted_iota(jnp.int32, (8, 128), 0)
    return both[0:8] & 127, jnp.where(slot < count, step, 9), both[8:16], 1.0 / count[0:1].astype(jnp.float32)


def write_picks(table_ref, half, odd, pick_ref, at):
    lane, step, code, inv = half_table(table_ref, half, odd)
    source = lax.broadcasted_iota(jnp.int32, (128, 128), 0)
    for i, d in enumerate(REACH[half]):
        wanted = jnp.where(step == d, lane, -1)
        for k in range(8):
            pick = (source == wanted[k : k + 1]).astype(jnp.float32).astype(jnp.bfloat16)
            pick_ref[k // 2, at + i, :, 128 * (k % 2) : 128 * (k % 2) + 128] = pick
    return code, inv


def tables_kernel(
    place_ref, own_ref, helmholtz_hbm, inverse_hbm,
    pick_ref, code_ref, weight_ref, inv_ref, high_ref, low_ref, helmholtz_ref, inverse_ref, sems,
):
    copies = fetch(((helmholtz_hbm, helmholtz_ref), (inverse_hbm, inverse_ref)), sems)
    odd = place_ref[0] == 1
    for half in (0, 1):
        code, inv = write_picks(own_ref, half, odd, pick_ref, 3 * half)
        code_ref[half] = code
        inv_ref[half] = jnp.broadcast_to(inv, (8, 128))
    for copy in copies:
        copy.wait()
    rows = lax.broadcasted_iota(jnp.int32, (16, 128), 0)
    lanes = lax.broadcasted_iota(jnp.int32, (16, 128), 1)
    coeff = jnp.sum(jnp.where(lanes == rows + 16 * place_ref[1], helmholtz_ref[...], 0.0), axis=1, keepdims=True)
    weight_ref[...] = jnp.broadcast_to(coeff / (1.0 + coeff), (16, 128))
    big = lax.broadcasted_iota(jnp.int32, (256, 16), 0) // 16 == lax.broadcasted_iota(jnp.int32, (256, 16), 1)
    rise = big.astype(jnp.float32).astype(jnp.bfloat16)
    wide = lax.broadcasted_iota(jnp.int32, (16, 256), 1) // 16 == lax.broadcasted_iota(jnp.int32, (16, 256), 0)
    spread = wide.astype(jnp.float32).astype(jnp.bfloat16)
    same = (
        lax.broadcasted_iota(jnp.int32, (256, 256), 0) % 16 == lax.broadcasted_iota(jnp.int32, (256, 256), 1) % 16
    )
    for ref, part in zip((high_ref, low_ref), split(inverse_ref[...])):
        ref[...] = jnp.where(same, dot(dot(rise, part).astype(jnp.bfloat16), spread), 0.0).astype(jnp.bfloat16)


def neighbor_sum(split_ref, first, count, pick_ref, at, code):
    total = [[None] * 16 for _ in range(2)]
    lhs = split_ref[:, 256 * first : 256 * (first + count)]
    for pair in range(4):
        rhs = jnp.concatenate([pick_ref[pair, at + c // 2] for c in range(2 * count)], axis=0)
        found = dot(lhs, rhs)
        for side in range(2):
            code_k = jnp.broadcast_to(code[2 * pair + side : 2 * pair + side + 1], (8, 128))
            swap = (code_k & 1) == 1
            flip_row = (code_k & 2) == 2
            flip_col = (code_k & 4) == 4
            for m in range(2):
                x = [found[16 * p + 8 * m : 16 * p + 8 * m + 8, 128 * side : 128 * side + 128] for p in range(16)]
                x = [jnp.where(flip_row, x[4 * (3 - i) + j], x[4 * i + j]) for i in range(4) for j in range(4)]
                x = [jnp.where(flip_col, x[4 * i + 3 - j], x[4 * i + j]) for i in range(4) for j in range(4)]
                x = [x[5 * i] if i == j else jnp.where(swap, x[4 * j + i], x[4 * i + j]) for i in range(4) for j in range(4)]
                total[m] = [v if t is None else t + v for t, v in zip(total[m], x)]
    return total


def fix(high_ref, low_ref, x):
    xh, xl = split(x)
    return dot(high_ref[...], xh) + (dot(high_ref[...], xl) + dot(low_ref[...], xh))


def sweep_kernel(
    place_ref, x_ref, source_table_ref, target_table_ref, pick_ref, code_ref, weight_ref, inv_ref, high_ref, low_ref,
    out_ref, u_ref, w_ref, us_ref, ws_ref, s_ref, other_ref,
):
    odd = place_ref[0] == 1
    known = {half: (code_ref[half], inv_ref[half]) for half in OWN}
    for half in OTHER:
        table_ref = source_table_ref if half == 2 else target_table_ref
        known[half] = write_picks(table_ref, half, odd, other_ref, OTHER[half])
    for half in range(4):
        base = 4 * jnp.where(odd, 3 - half, half)
        for quad in range(4):
            parts = [x_ref[base + j, 16 * quad : 16 * quad + 16, :] for j in range(4)]
            for i, part in enumerate(transpose_quads(parts)):
                rows = slice(64 * quad + 16 * i, 64 * quad + 16 * i + 16)
                u_ref[half, rows, :] = part
                high, low = split(part)
                us_ref[rows, 256 * half : 256 * half + 128] = high
                us_ref[rows, 256 * half + 128 : 256 * half + 256] = low
    for place, half in enumerate((-1, 0, 1, 2)):
        steps = [d for d in REACH[half] if 0 <= half + d <= 3]
        picks, at = (pick_ref, OWN[half]) if half in OWN else (other_ref, OTHER[half])
        code, inv = known[half]
        total = neighbor_sum(us_ref, half + steps[0], len(steps), picks, at + REACH[half].index(steps[0]), code)
        for m in range(2):
            weight = weight_ref[8 * m : 8 * m + 8, :] * inv
            for p in range(16):
                s_ref[16 * p + 8 * m : 16 * p + 8 * m + 8, 128 * place : 128 * place + 128] = weight * total[m][p]
    fixed = fix(high_ref, low_ref, s_ref[...])
    for place in range(4):
        part = fixed[:, 128 * place : 128 * place + 128]
        w_ref[place] = part
        high, low = split(part)
        ws_ref[:, 256 * place : 256 * place + 128] = high
        ws_ref[:, 256 * place + 128 : 256 * place + 256] = low
    for place, half in enumerate((-2, -1, 0, 1)):
        steps = [d for d in REACH[half] if -1 <= half + d <= 2]
        picks, at = (pick_ref, OWN[half]) if half in OWN else (other_ref, OTHER[half])
        code, inv = known[half]
        total = neighbor_sum(ws_ref, half + steps[0] + 1, len(steps), picks, at + REACH[half].index(steps[0]), code)
        for m in range(2):
            weight = weight_ref[8 * m : 8 * m + 8, :] * inv
            for p in range(16):
                rows = slice(16 * p + 8 * m, 16 * p + 8 * m + 8)
                value = weight * total[m][p]
                if half >= -1:
                    value = value - w_ref[half + 1, rows, :]
                s_ref[rows, 128 * place : 128 * place + 128] = value
    fixed = fix(high_ref, low_ref, s_ref[...])
    for place, half in enumerate((-2, -1, 0, 1)):
        base = 4 * jnp.where(odd, 3 - place, place)
        for quad in range(4):
            parts = []
            for i in range(4):
                rows = slice(64 * quad + 16 * i, 64 * quad + 16 * i + 16)
                value = fixed[rows, 128 * place : 128 * place + 128]
                if half >= -1:
                    value = value + 2.0 * w_ref[half + 1, rows, :]
                if half >= 0:
                    value = value + u_ref[half, rows, :]
                parts.append(value)
            for j, part in enumerate(transpose_quads(parts)):
                out_ref[base + j, 16 * quad : 16 * quad + 16, :] = part


def to_levels_kernel(parts_ref, levels_ref, out_ref, modes_ref):
    for group in range(8):
        for quad in range(4):
            rows = slice(16 * quad, 16 * quad + 16)
            modes_ref[16 * group : 16 * group + 16, 128 * quad : 128 * quad + 128] = (
                parts_ref[group, rows, :] + parts_ref[8 + group, rows, :]
            )
    high, low = split(dot3(levels_ref[...], modes_ref[...]))
    row = lax.broadcasted_iota(jnp.int32, (512, 512), 0)
    col = lax.broadcasted_iota(jnp.int32, (1, 512), 1)
    perm = (row == (col % 16) * 32 + col // 16).astype(jnp.float32).astype(jnp.bfloat16)
    out_ref[...] = dot(high, perm) + dot(low, perm)


def cost(flops, moved):
    return pl.CostEstimate(flops=flops, bytes_accessed=moved, transcendentals=0)


def near(x):
    return pltpu.with_memory_space_constraint(x, pltpu.VMEM)


def far(x):
    return pltpu.with_memory_space_constraint(x, pltpu.HBM)


VMEM = pl.BlockSpec(memory_space=pltpu.VMEM)
SMEM = pl.BlockSpec(memory_space=pltpu.SMEM)
HBM = pl.BlockSpec(memory_space=pltpu.HBM)
LIMIT = pltpu.CompilerParams(vmem_limit_bytes=20 << 20)


def body(blocks, levels_rhs, to_modes, from_modes, helmholtz, local_inverse, neighbor_ids, neighbor_count, orientation):
    axes = ("elem", "mode")
    parts = lax.axis_size("mode")
    source_pairs = [
        [((2 * k - 1 + i) % blocks) * parts + j for i in range(2) for j in range(parts)] for k in range(blocks // 2)
    ]
    target_pairs = [[(2 * k + i) * parts + j for i in range(2) for j in range(parts)] for k in range(blocks // 2)]
    source_swap = [(b, (((b + 1) ^ 1) - 1) % blocks) for b in range(blocks)]
    target_swap = [(b, b ^ 1) for b in range(blocks)]
    helmholtz = helmholtz[None]
    place = jnp.stack([(lax.axis_index("elem") + 1) % 2, lax.axis_index("mode")]).astype(jnp.int32)

    start, own = pl.pallas_call(
        to_modes_kernel,
        out_shape=(pltpu.VMEM((16, 64, 128), jnp.float32), pltpu.VMEM((24, 256), jnp.int32)),
        in_specs=[HBM] * 6,
        out_specs=(VMEM, VMEM),
        scratch_shapes=[
            pltpu.VMEM((128, 512), jnp.float32),
            pltpu.VMEM((128, 128), jnp.float32),
            pltpu.VMEM((1, 128), jnp.float32),
            pltpu.VMEM((1, 256), jnp.int32),
            pltpu.SemaphoreType.DMA((6,)),
        ],
        compiler_params=LIMIT,
        cost_estimate=cost(2 * 128 * 512 * (512 + 128), 1 << 20),
        name="to_modes_chunks",
    )(*[far(x) for x in (levels_rhs, to_modes, helmholtz, neighbor_ids, orientation, neighbor_count[None])])
    sources = lax.all_to_all(start, axes, 0, 0, axis_index_groups=source_pairs, tiled=True)
    target_table = lax.ppermute(own, "elem", target_swap)
    source_table = lax.ppermute(own, "elem", source_swap)
    parts_of_tables = pl.pallas_call(
        tables_kernel,
        out_shape=(
            pltpu.VMEM((4, 6, 128, 256), jnp.bfloat16),
            pltpu.VMEM((2, 8, 128), jnp.int32),
            pltpu.VMEM((16, 128), jnp.float32),
            pltpu.VMEM((2, 8, 128), jnp.float32),
            pltpu.VMEM((256, 256), jnp.bfloat16),
            pltpu.VMEM((256, 256), jnp.bfloat16),
        ),
        in_specs=[SMEM, VMEM, HBM, HBM],
        out_specs=(VMEM,) * 6,
        scratch_shapes=[
            pltpu.VMEM((1, 128), jnp.float32),
            pltpu.VMEM((16, 16), jnp.float32),
            pltpu.SemaphoreType.DMA((2,)),
        ],
        compiler_params=LIMIT,
        cost_estimate=cost(1 << 28, 2 << 20),
        name="own_tables",
    )(place, near(own), far(helmholtz), far(local_inverse))
    targets = pl.pallas_call(
        sweep_kernel,
        out_shape=pltpu.VMEM((16, 64, 128), jnp.float32),
        in_specs=[SMEM] + [VMEM] * 9,
        out_specs=VMEM,
        scratch_shapes=[
            pltpu.VMEM((4, 256, 128), jnp.float32),
            pltpu.VMEM((4, 256, 128), jnp.float32),
            pltpu.VMEM((256, 1024), jnp.bfloat16),
            pltpu.VMEM((256, 1024), jnp.bfloat16),
            pltpu.VMEM((256, 512), jnp.float32),
            pltpu.VMEM((4, 6, 128, 256), jnp.bfloat16),
        ],
        compiler_params=LIMIT,
        cost_estimate=cost(4 << 30, 8 << 20),
        name="two_sweeps",
    )(place, near(sources), near(source_table), near(target_table), *[near(part) for part in parts_of_tables])
    whole = lax.all_to_all(targets, axes, 0, 0, axis_index_groups=target_pairs, tiled=True)
    return pl.pallas_call(
        to_levels_kernel,
        out_shape=jax.ShapeDtypeStruct((128, 512), jnp.float32),
        in_specs=[VMEM] * 2,
        out_specs=VMEM,
        scratch_shapes=[pltpu.VMEM((128, 512), jnp.float32)],
        compiler_params=LIMIT,
        cost_estimate=cost(2 * 128 * 512 * (512 + 128), 1 << 20),
        name="to_levels",
    )(near(whole), from_modes)


def solution(mesh):
    in_specs = (
        P(None, ("elem", "mode")),
        P(),
        P(),
        P(),
        P(),
        P(None, "elem"),
        P("elem"),
        P(None, "elem"),
    )
    out_specs = P(None, ("elem", "mode"))
    return jax.shard_map(
        functools.partial(body, mesh.shape["elem"]), mesh=mesh, in_specs=in_specs, out_specs=out_specs, check_vma=False
    )
```

```python
import functools

import jax
import jax.numpy as jnp
from jax import lax
from jax.experimental import pallas as pl
from jax.experimental.pallas import tpu as pltpu
from jax.sharding import PartitionSpec as P


def split(x):
    high = x.astype(jnp.bfloat16)
    return high, (x - high.astype(jnp.float32)).astype(jnp.bfloat16)


def dot(a, b):
    return jnp.dot(a, b, preferred_element_type=jnp.float32)


def dot3(a, b):
    ah, al = split(a)
    bh, bl = split(b)
    return dot(ah, bh) + (dot(ah, bl) + dot(al, bh))


def column(row):
    count = row.shape[1]
    at = lax.broadcasted_iota(jnp.int32, (count, count), 0) == lax.broadcasted_iota(jnp.int32, (count, count), 1)
    return jnp.sum(jnp.where(at, row, 0.0), axis=1, keepdims=True)


def fetch(pairs, sems):
    copies = [pltpu.make_async_copy(src, dst, sems.at[i]) for i, (src, dst) in enumerate(pairs)]
    for copy in copies:
        copy.start()
    return copies


def to_modes_kernel(
    rhs_hbm, modes_hbm, helmholtz_hbm, ids_hbm, orientation_hbm, count_hbm,
    out_ref, table_ref, rhs_ref, modes_ref, helmholtz_ref, count_ref, sems,
):
    copies = fetch(
        (
            (rhs_hbm, rhs_ref),
            (modes_hbm, modes_ref),
            (helmholtz_hbm, helmholtz_ref),
            (ids_hbm, table_ref.at[0:8]),
            (orientation_hbm, table_ref.at[8:16]),
            (count_hbm, count_ref),
        ),
        sems,
    )
    row = lax.broadcasted_iota(jnp.int32, (512, 512), 0)
    col = lax.broadcasted_iota(jnp.int32, (1, 512), 1)
    perm = (row == (col % 32) * 16 + col // 32).astype(jnp.float32).astype(jnp.bfloat16)
    for copy in copies:
        copy.wait()
    table_ref[16:24] = jnp.broadcast_to(count_ref[...], (8, 256))
    high, low = split(rhs_ref[...])
    high = dot(high, perm).astype(jnp.bfloat16)
    low = dot(low, perm).astype(jnp.bfloat16)
    mh, ml = split(modes_ref[...] * column(1.0 / (1.0 + helmholtz_ref[...])))
    start = dot(mh, high) + (dot(mh, low) + dot(ml, high))
    for group in range(8):
        for quad in range(4):
            part = start[16 * group : 16 * group + 16, 128 * quad : 128 * quad + 128]
            for copy in range(2):
                out_ref[8 * copy + group, 16 * quad : 16 * quad + 16, :] = part


def transpose_quads(parts):
    rows = parts[0].shape[0]
    where_at = lax.broadcasted_iota(jnp.int32, (rows, 128), 1) // 32
    outs = []
    for i in range(4):
        out = None
        for j in range(4):
            shift = (32 * (j - i)) % 128
            moved = parts[j] if shift == 0 else pltpu.roll(parts[j], shift, 1)
            out = moved if out is None else jnp.where(where_at == j, moved, out)
        outs.append(out)
    return outs


REACH = {-2: (1,), -1: (0, 1), 0: (-1, 0, 1), 1: (-1, 0, 1), 2: (-1, 0, 1)}
OWN = {0: 0, 1: 3}
OTHER = {-2: 0, -1: 1, 2: 3}


def half_table(table_ref, half, odd):
    even_half, odd_half = half % 2, (half + 1) % 2
    even = table_ref[:, 128 * even_half : 128 * even_half + 128]
    other = table_ref[:, 128 * odd_half : 128 * odd_half + 128]
    step = jnp.where(odd, 1 + odd_half - (other[0:8] >> 7), (even[0:8] >> 7) - 1 - even_half)
    both = jnp.where(odd, other, even)
    count = both[16:24]
    slot = lax.broadcasted_iota(jnp.int32, (8, 128), 0)
    return both[0:8] & 127, jnp.where(slot < count, step, 9), both[8:16], 1.0 / count[0:1].astype(jnp.float32)


def write_picks(table_ref, half, odd, pick_ref, at):
    lane, step, code, inv = half_table(table_ref, half, odd)
    source = lax.broadcasted_iota(jnp.int32, (128, 128), 0)
    for i, d in enumerate(REACH[half]):
        wanted = jnp.where(step == d, lane, -1)
        for k in range(8):
            pick = (source == wanted[k : k + 1]).astype(jnp.float32).astype(jnp.bfloat16)
            pick_ref[k // 2, at + i, :, 128 * (k % 2) : 128 * (k % 2) + 128] = pick
    return code, inv


def tables_kernel(
    place_ref, own_ref, helmholtz_hbm, inverse_hbm,
    pick_ref, code_ref, weight_ref, inv_ref, high_ref, low_ref, helmholtz_ref, inverse_ref, sems,
):
    copies = fetch(((helmholtz_hbm, helmholtz_ref), (inverse_hbm, inverse_ref)), sems)
    odd = place_ref[0] == 1
    for half in (0, 1):
        code, inv = write_picks(own_ref, half, odd, pick_ref, 3 * half)
        code_ref[half] = code
        inv_ref[half] = jnp.broadcast_to(inv, (8, 128))
    for copy in copies:
        copy.wait()
    rows = lax.broadcasted_iota(jnp.int32, (16, 128), 0)
    lanes = lax.broadcasted_iota(jnp.int32, (16, 128), 1)
    coeff = jnp.sum(jnp.where(lanes == rows + 16 * place_ref[1], helmholtz_ref[...], 0.0), axis=1, keepdims=True)
    weight_ref[...] = jnp.broadcast_to(coeff / (1.0 + coeff), (16, 128))
    big = lax.broadcasted_iota(jnp.int32, (256, 16), 0) // 16 == lax.broadcasted_iota(jnp.int32, (256, 16), 1)
    rise = big.astype(jnp.float32).astype(jnp.bfloat16)
    wide = lax.broadcasted_iota(jnp.int32, (16, 256), 1) // 16 == lax.broadcasted_iota(jnp.int32, (16, 256), 0)
    spread = wide.astype(jnp.float32).astype(jnp.bfloat16)
    same = (
        lax.broadcasted_iota(jnp.int32, (256, 256), 0) % 16 == lax.broadcasted_iota(jnp.int32, (256, 256), 1) % 16
    )
    for ref, part in zip((high_ref, low_ref), split(inverse_ref[...])):
        ref[...] = jnp.where(same, dot(dot(rise, part).astype(jnp.bfloat16), spread), 0.0).astype(jnp.bfloat16)


def neighbor_sum(split_ref, first, count, pick_ref, at, code):
    total = [[None] * 16 for _ in range(2)]
    lhs = split_ref[:, 256 * first : 256 * (first + count)]
    for pair in range(4):
        rhs = jnp.concatenate([pick_ref[pair, at + c // 2] for c in range(2 * count)], axis=0)
        found = dot(lhs, rhs)
        for side in range(2):
            code_k = jnp.broadcast_to(code[2 * pair + side : 2 * pair + side + 1], (8, 128))
            swap = (code_k & 1) == 1
            flip_row = (code_k & 2) == 2
            flip_col = (code_k & 4) == 4
            for m in range(2):
                x = [found[16 * p + 8 * m : 16 * p + 8 * m + 8, 128 * side : 128 * side + 128] for p in range(16)]
                x = [jnp.where(flip_row, x[4 * (3 - i) + j], x[4 * i + j]) for i in range(4) for j in range(4)]
                x = [jnp.where(flip_col, x[4 * i + 3 - j], x[4 * i + j]) for i in range(4) for j in range(4)]
                x = [x[5 * i] if i == j else jnp.where(swap, x[4 * j + i], x[4 * i + j]) for i in range(4) for j in range(4)]
                total[m] = [v if t is None else t + v for t, v in zip(total[m], x)]
    return total


def fix(high_ref, low_ref, x):
    xh, xl = split(x)
    return dot(high_ref[...], xh) + (dot(high_ref[...], xl) + dot(low_ref[...], xh))


def sweep_kernel(
    place_ref, x_ref, target_table_ref, source_table_ref, pick_ref, code_ref, weight_ref, inv_ref, high_ref, low_ref,
    out_ref, u_ref, w_ref, us_ref, ws_ref, s_ref, other_ref,
):
    odd = place_ref[0] == 1
    known = {half: (code_ref[half], inv_ref[half]) for half in OWN}
    for half in OTHER:
        table_ref = source_table_ref if half == 2 else target_table_ref
        known[half] = write_picks(table_ref, half, odd, other_ref, OTHER[half])
    for half in range(4):
        base = 4 * jnp.where(odd, 3 - half, half)
        for quad in range(4):
            parts = [x_ref[base + j, 16 * quad : 16 * quad + 16, :] for j in range(4)]
            for i, part in enumerate(transpose_quads(parts)):
                rows = slice(64 * quad + 16 * i, 64 * quad + 16 * i + 16)
                u_ref[half, rows, :] = part
                high, low = split(part)
                us_ref[rows, 256 * half : 256 * half + 128] = high
                us_ref[rows, 256 * half + 128 : 256 * half + 256] = low
    for place, half in enumerate((-1, 0, 1, 2)):
        steps = [d for d in REACH[half] if 0 <= half + d <= 3]
        picks, at = (pick_ref, OWN[half]) if half in OWN else (other_ref, OTHER[half])
        code, inv = known[half]
        total = neighbor_sum(us_ref, half + steps[0], len(steps), picks, at + REACH[half].index(steps[0]), code)
        for m in range(2):
            weight = weight_ref[8 * m : 8 * m + 8, :] * inv
            for p in range(16):
                s_ref[16 * p + 8 * m : 16 * p + 8 * m + 8, 128 * place : 128 * place + 128] = weight * total[m][p]
    fixed = fix(high_ref, low_ref, s_ref[...])
    for place in range(4):
        part = fixed[:, 128 * place : 128 * place + 128]
        w_ref[place] = part
        high, low = split(part)
        ws_ref[:, 256 * place : 256 * place + 128] = high
        ws_ref[:, 256 * place + 128 : 256 * place + 256] = low
    for place, half in enumerate((-2, -1, 0, 1)):
        steps = [d for d in REACH[half] if -1 <= half + d <= 2]
        picks, at = (pick_ref, OWN[half]) if half in OWN else (other_ref, OTHER[half])
        code, inv = known[half]
        total = neighbor_sum(ws_ref, half + steps[0] + 1, len(steps), picks, at + REACH[half].index(steps[0]), code)
        for m in range(2):
            weight = weight_ref[8 * m : 8 * m + 8, :] * inv
            for p in range(16):
                rows = slice(16 * p + 8 * m, 16 * p + 8 * m + 8)
                value = weight * total[m][p]
                if half >= -1:
                    value = value - w_ref[half + 1, rows, :]
                s_ref[rows, 128 * place : 128 * place + 128] = value
    fixed = fix(high_ref, low_ref, s_ref[...])
    for place, half in enumerate((-2, -1, 0, 1)):
        base = 4 * jnp.where(odd, 3 - place, place)
        for quad in range(4):
            parts = []
            for i in range(4):
                rows = slice(64 * quad + 16 * i, 64 * quad + 16 * i + 16)
                value = fixed[rows, 128 * place : 128 * place + 128]
                if half >= -1:
                    value = value + 2.0 * w_ref[half + 1, rows, :]
                if half >= 0:
                    value = value + u_ref[half, rows, :]
                parts.append(value)
            for j, part in enumerate(transpose_quads(parts)):
                out_ref[base + j, 16 * quad : 16 * quad + 16, :] = part


def to_levels_kernel(parts_ref, levels_ref, out_ref, modes_ref):
    for group in range(8):
        for quad in range(4):
            rows = slice(16 * quad, 16 * quad + 16)
            modes_ref[16 * group : 16 * group + 16, 128 * quad : 128 * quad + 128] = (
                parts_ref[group, rows, :] + parts_ref[8 + group, rows, :]
            )
    high, low = split(dot3(levels_ref[...], modes_ref[...]))
    row = lax.broadcasted_iota(jnp.int32, (512, 512), 0)
    col = lax.broadcasted_iota(jnp.int32, (1, 512), 1)
    perm = (row == (col % 16) * 32 + col // 16).astype(jnp.float32).astype(jnp.bfloat16)
    out_ref[...] = dot(high, perm) + dot(low, perm)


def cost(flops, moved):
    return pl.CostEstimate(flops=flops, bytes_accessed=moved, transcendentals=0)


def near(x):
    return pltpu.with_memory_space_constraint(x, pltpu.VMEM)


def far(x):
    return pltpu.with_memory_space_constraint(x, pltpu.HBM)


VMEM = pl.BlockSpec(memory_space=pltpu.VMEM)
SMEM = pl.BlockSpec(memory_space=pltpu.SMEM)
HBM = pl.BlockSpec(memory_space=pltpu.HBM)
LIMIT = pltpu.CompilerParams(vmem_limit_bytes=20 << 20)


def body(blocks, levels_rhs, to_modes, from_modes, helmholtz, local_inverse, neighbor_ids, neighbor_count, orientation):
    axes = ("elem", "mode")
    parts = lax.axis_size("mode")
    source_pairs = [
        [((2 * k - 1 + i) % blocks) * parts + j for i in range(2) for j in range(parts)] for k in range(blocks // 2)
    ]
    target_pairs = [[(2 * k + i) * parts + j for i in range(2) for j in range(parts)] for k in range(blocks // 2)]
    source_swap = [(b, (((b + 1) ^ 1) - 1) % blocks) for b in range(blocks)]
    target_swap = [(b, b ^ 1) for b in range(blocks)]
    helmholtz = helmholtz[None]
    place = jnp.stack([(lax.axis_index("elem") + 1) % 2, lax.axis_index("mode")]).astype(jnp.int32)

    start, own = pl.pallas_call(
        to_modes_kernel,
        out_shape=(pltpu.VMEM((16, 64, 128), jnp.float32), pltpu.VMEM((24, 256), jnp.int32)),
        in_specs=[HBM] * 6,
        out_specs=(VMEM, VMEM),
        scratch_shapes=[
            pltpu.VMEM((128, 512), jnp.float32),
            pltpu.VMEM((128, 128), jnp.float32),
            pltpu.VMEM((1, 128), jnp.float32),
            pltpu.VMEM((1, 256), jnp.int32),
            pltpu.SemaphoreType.DMA((6,)),
        ],
        compiler_params=LIMIT,
        cost_estimate=cost(2 * 128 * 512 * (512 + 128), 1 << 20),
        name="to_modes_chunks",
    )(*[far(x) for x in (levels_rhs, to_modes, helmholtz, neighbor_ids, orientation, neighbor_count[None])])
    sources = lax.all_to_all(start, axes, 0, 0, axis_index_groups=source_pairs, tiled=True)
    source_table = lax.ppermute(own, "elem", source_swap)
    target_table = lax.ppermute(own, "elem", target_swap)
    parts_of_tables = pl.pallas_call(
        tables_kernel,
        out_shape=(
            pltpu.VMEM((4, 6, 128, 256), jnp.bfloat16),
            pltpu.VMEM((2, 8, 128), jnp.int32),
            pltpu.VMEM((16, 128), jnp.float32),
            pltpu.VMEM((2, 8, 128), jnp.float32),
            pltpu.VMEM((256, 256), jnp.bfloat16),
            pltpu.VMEM((256, 256), jnp.bfloat16),
        ),
        in_specs=[SMEM, VMEM, HBM, HBM],
        out_specs=(VMEM,) * 6,
        scratch_shapes=[
            pltpu.VMEM((1, 128), jnp.float32),
            pltpu.VMEM((16, 16), jnp.float32),
            pltpu.SemaphoreType.DMA((2,)),
        ],
        compiler_params=LIMIT,
        cost_estimate=cost(1 << 28, 2 << 20),
        name="own_tables",
    )(place, near(own), far(helmholtz), far(local_inverse))
    targets = pl.pallas_call(
        sweep_kernel,
        out_shape=pltpu.VMEM((16, 64, 128), jnp.float32),
        in_specs=[SMEM] + [VMEM] * 9,
        out_specs=VMEM,
        scratch_shapes=[
            pltpu.VMEM((4, 256, 128), jnp.float32),
            pltpu.VMEM((4, 256, 128), jnp.float32),
            pltpu.VMEM((256, 1024), jnp.bfloat16),
            pltpu.VMEM((256, 1024), jnp.bfloat16),
            pltpu.VMEM((256, 512), jnp.float32),
            pltpu.VMEM((4, 6, 128, 256), jnp.bfloat16),
        ],
        compiler_params=LIMIT,
        cost_estimate=cost(4 << 30, 8 << 20),
        name="two_sweeps",
    )(place, near(sources), near(target_table), near(source_table), *[near(part) for part in parts_of_tables])
    whole = lax.all_to_all(targets, axes, 0, 0, axis_index_groups=target_pairs, tiled=True)
    return pl.pallas_call(
        to_levels_kernel,
        out_shape=jax.ShapeDtypeStruct((128, 512), jnp.float32),
        in_specs=[VMEM] * 2,
        out_specs=VMEM,
        scratch_shapes=[pltpu.VMEM((128, 512), jnp.float32)],
        compiler_params=LIMIT,
        cost_estimate=cost(2 * 128 * 512 * (512 + 128), 1 << 20),
        name="to_levels",
    )(near(whole), from_modes)


def solution(mesh):
    in_specs = (
        P(None, ("elem", "mode")),
        P(),
        P(),
        P(),
        P(),
        P(None, "elem"),
        P("elem"),
        P(None, "elem"),
    )
    out_specs = P(None, ("elem", "mode"))
    return jax.shard_map(
        functools.partial(body, mesh.shape["elem"]), mesh=mesh, in_specs=in_specs, out_specs=out_specs, check_vma=False
    )
```

```python
import functools

import jax
import jax.numpy as jnp
from jax import lax
from jax.experimental import pallas as pl
from jax.experimental.pallas import tpu as pltpu
from jax.sharding import PartitionSpec as P


def split(x):
    high = x.astype(jnp.bfloat16)
    return high, (x - high.astype(jnp.float32)).astype(jnp.bfloat16)


def dot(a, b):
    return jnp.dot(a, b, preferred_element_type=jnp.float32)


def dot3(a, b):
    ah, al = split(a)
    bh, bl = split(b)
    return dot(ah, bh) + (dot(ah, bl) + dot(al, bh))


def point_keys(index, spread):
    if spread:
        e, p = index >> 4, index & 15
        i, j = p >> 2, p & 3
        high_i, high_j = i >> 1, j >> 1
        a = jnp.where(high_i == 1, 3 - i, i)
        b = jnp.where(high_j == 1, 3 - j, j)
        return e * 4 + a * 2 + b, high_i * 2 + high_j
    t, e = index >> 5, index & 31
    return e * 4 + (t & 3), t >> 2


def parity_matrix(t, p, scale):
    i, j = p >> 2, p & 3
    near = jnp.where(i > 1, 3 - i, i) * 2 + jnp.where(j > 1, 3 - j, j)
    odd = ((i >> 1) * 2 + (j >> 1)) & (t >> 2)
    value = jnp.where((odd == 1) | (odd == 2), -scale, scale)
    return jnp.where(near == (t & 3), value, 0.0).astype(jnp.bfloat16)


def point_matrix(row_points, scale):
    row, row_bits = point_keys(lax.broadcasted_iota(jnp.int32, (512, 1), 0), row_points)
    col, col_bits = point_keys(lax.broadcasted_iota(jnp.int32, (1, 512), 1), not row_points)
    odd = row_bits & col_bits
    value = jnp.where((odd == 1) | (odd == 2), -scale, scale)
    return jnp.where(row == col, value, 0.0).astype(jnp.bfloat16)


def column(row):
    count = row.shape[1]
    at = lax.broadcasted_iota(jnp.int32, (count, count), 0) == lax.broadcasted_iota(jnp.int32, (count, count), 1)
    return jnp.sum(jnp.where(at, row, 0.0), axis=1, keepdims=True)


def fetch(pairs, sems):
    copies = [pltpu.make_async_copy(src, dst, sems.at[i]) for i, (src, dst) in enumerate(pairs)]
    for copy in copies:
        copy.start()
    return copies


def to_modes_kernel(
    rhs_hbm, modes_hbm, helmholtz_hbm, ids_hbm, orientation_hbm, count_hbm,
    out_ref, table_ref, rhs_ref, modes_ref, helmholtz_ref, count_ref, sems,
):
    copies = fetch(
        (
            (rhs_hbm, rhs_ref),
            (modes_hbm, modes_ref),
            (helmholtz_hbm, helmholtz_ref),
            (ids_hbm, table_ref.at[0:8]),
            (orientation_hbm, table_ref.at[8:16]),
            (count_hbm, count_ref),
        ),
        sems,
    )
    points = point_matrix(True, 1.0)
    for copy in copies:
        copy.wait()
    table_ref[16:24] = jnp.broadcast_to(count_ref[...], (8, 256))
    high, low = split(rhs_ref[...])
    high, low = split(dot(high, points) + dot(low, points))
    mh, ml = split(modes_ref[...] * column(1.0 / (1.0 + helmholtz_ref[...])))
    start = dot(mh, high) + (dot(mh, low) + dot(ml, high))
    for group in range(8):
        for quad in range(4):
            part = start[16 * group : 16 * group + 16, 128 * quad : 128 * quad + 128]
            for copy in range(2):
                out_ref[8 * copy + group, 16 * quad : 16 * quad + 16, :] = part


def transpose_quads(parts):
    rows = parts[0].shape[0]
    where_at = lax.broadcasted_iota(jnp.int32, (rows, 128), 1) // 32
    outs = []
    for i in range(4):
        out = None
        for j in range(4):
            shift = (32 * (j - i)) % 128
            moved = parts[j] if shift == 0 else pltpu.roll(parts[j], shift, 1)
            out = moved if out is None else jnp.where(where_at == j, moved, out)
        outs.append(out)
    return outs


REACH = {-2: (1,), -1: (0, 1), 0: (-1, 0, 1), 1: (-1, 0, 1), 2: (-1, 0, 1)}
OWN = {0: 0, 1: 3}
OTHER = {-2: 0, -1: 1, 2: 3}


def half_table(table_ref, half, odd):
    even_half, odd_half = half % 2, (half + 1) % 2
    even = table_ref[:, 128 * even_half : 128 * even_half + 128]
    other = table_ref[:, 128 * odd_half : 128 * odd_half + 128]
    step = jnp.where(odd, 1 + odd_half - (other[0:8] >> 7), (even[0:8] >> 7) - 1 - even_half)
    both = jnp.where(odd, other, even)
    count = both[16:24]
    slot = lax.broadcasted_iota(jnp.int32, (8, 128), 0)
    return both[0:8] & 127, jnp.where(slot < count, step, 9), both[8:16], 1.0 / count[0:1].astype(jnp.float32)


def write_picks(table_ref, half, odd, pick_ref, at):
    lane, step, code, inv = half_table(table_ref, half, odd)
    source = lax.broadcasted_iota(jnp.int32, (128, 128), 0)
    for i, d in enumerate(REACH[half]):
        wanted = jnp.where(step == d, lane, -1)
        for k in range(8):
            pick = (source == wanted[k : k + 1]).astype(jnp.float32).astype(jnp.bfloat16)
            pick_ref[k // 2, at + i, :, 128 * (k % 2) : 128 * (k % 2) + 128] = pick
    return code, inv


def tables_kernel(
    place_ref, own_ref, helmholtz_hbm, inverse_hbm,
    pick_ref, code_ref, weight_ref, inv_ref, high_ref, low_ref, back_ref, helmholtz_ref, inverse_ref, sems,
):
    copies = fetch(((helmholtz_hbm, helmholtz_ref), (inverse_hbm, inverse_ref)), sems)
    odd = place_ref[0] == 1
    for half in (0, 1):
        code, inv = write_picks(own_ref, half, odd, pick_ref, 3 * half)
        code_ref[half] = code
        inv_ref[half] = jnp.broadcast_to(inv, (8, 128))
    for copy in copies:
        copy.wait()
    back_ref[...] = point_matrix(False, 0.25)
    rows = lax.broadcasted_iota(jnp.int32, (16, 128), 0)
    lanes = lax.broadcasted_iota(jnp.int32, (16, 128), 1)
    coeff = jnp.sum(jnp.where(lanes == rows + 16 * place_ref[1], helmholtz_ref[...], 0.0), axis=1, keepdims=True)
    weight_ref[...] = jnp.broadcast_to(coeff / (1.0 + coeff), (16, 128))
    big = lax.broadcasted_iota(jnp.int32, (256, 16), 0) // 16 == lax.broadcasted_iota(jnp.int32, (256, 16), 1)
    rise = big.astype(jnp.float32).astype(jnp.bfloat16)
    wide = lax.broadcasted_iota(jnp.int32, (16, 256), 1) // 16 == lax.broadcasted_iota(jnp.int32, (16, 256), 0)
    spread = wide.astype(jnp.float32).astype(jnp.bfloat16)
    same = (
        lax.broadcasted_iota(jnp.int32, (256, 256), 0) % 16 == lax.broadcasted_iota(jnp.int32, (256, 256), 1) % 16
    )
    t = lax.broadcasted_iota(jnp.int32, (16, 16), 0)
    p = lax.broadcasted_iota(jnp.int32, (16, 16), 1)
    there = parity_matrix(t, p, 1.0)
    high, low = split(inverse_ref[...])
    high, low = split(dot(there, high) + dot(there, low))
    again = parity_matrix(p, t, 0.25)
    for ref, part in zip((high_ref, low_ref), split(dot(high, again) + dot(low, again))):
        ref[...] = jnp.where(same, dot(dot(rise, part).astype(jnp.bfloat16), spread), 0.0).astype(jnp.bfloat16)


def neighbor_sum(split_ref, first, count, pick_ref, at, code):
    total = [[None] * 16 for _ in range(2)]
    lhs = split_ref[:, 256 * first : 256 * (first + count)]
    for pair in range(4):
        rhs = jnp.concatenate([pick_ref[pair, at + c // 2] for c in range(2 * count)], axis=0)
        found = dot(lhs, rhs)
        for side in range(2):
            code_k = jnp.broadcast_to(code[2 * pair + side : 2 * pair + side + 1], (8, 128))
            swap = (code_k & 1) == 1
            by_row = jnp.where((code_k & 2) == 2, -1.0, 1.0)
            by_col = jnp.where((code_k & 4) == 4, -1.0, 1.0)
            by_both = by_row * by_col
            for m in range(2):
                x = [found[16 * p + 8 * m : 16 * p + 8 * m + 8, 128 * side : 128 * side + 128] for p in range(16)]
                even, col_odd, row_odd, odd = x[0:4], x[4:8], x[8:12], x[12:16]
                col_odd = [v * by_col for v in col_odd]
                row_odd = [v * by_row for v in row_odd]
                odd = [v * by_both for v in odd]
                turned = (0, 2, 1, 3)
                x = (
                    [even[i] if i == t else jnp.where(swap, even[t], even[i]) for i, t in enumerate(turned)]
                    + [jnp.where(swap, row_odd[t], col_odd[i]) for i, t in enumerate(turned)]
                    + [jnp.where(swap, col_odd[t], row_odd[i]) for i, t in enumerate(turned)]
                    + [odd[i] if i == t else jnp.where(swap, odd[t], odd[i]) for i, t in enumerate(turned)]
                )
                total[m] = [v if t is None else t + v for t, v in zip(total[m], x)]
    return total


def fix(high_ref, low_ref, x):
    xh, xl = split(x)
    return dot(high_ref[...], xh) + (dot(high_ref[...], xl) + dot(low_ref[...], xh))


def sweep_kernel(
    place_ref, x_ref, target_table_ref, source_table_ref, pick_ref, code_ref, weight_ref, inv_ref, high_ref, low_ref,
    out_ref, u_ref, w_ref, us_ref, ws_ref, s_ref, other_ref,
):
    odd = place_ref[0] == 1
    known = {half: (code_ref[half], inv_ref[half]) for half in OWN}
    for half in OTHER:
        table_ref = source_table_ref if half == 2 else target_table_ref
        known[half] = write_picks(table_ref, half, odd, other_ref, OTHER[half])
    for half in range(4):
        base = 4 * jnp.where(odd, 3 - half, half)
        for quad in range(4):
            parts = [x_ref[base + j, 16 * quad : 16 * quad + 16, :] for j in range(4)]
            for i, part in enumerate(transpose_quads(parts)):
                rows = slice(64 * quad + 16 * i, 64 * quad + 16 * i + 16)
                u_ref[half, rows, :] = part
                high, low = split(part)
                us_ref[rows, 256 * half : 256 * half + 128] = high
                us_ref[rows, 256 * half + 128 : 256 * half + 256] = low
    for place, half in enumerate((-1, 0, 1, 2)):
        steps = [d for d in REACH[half] if 0 <= half + d <= 3]
        picks, at = (pick_ref, OWN[half]) if half in OWN else (other_ref, OTHER[half])
        code, inv = known[half]
        total = neighbor_sum(us_ref, half + steps[0], len(steps), picks, at + REACH[half].index(steps[0]), code)
        for m in range(2):
            weight = weight_ref[8 * m : 8 * m + 8, :] * inv
            for p in range(16):
                s_ref[16 * p + 8 * m : 16 * p + 8 * m + 8, 128 * place : 128 * place + 128] = weight * total[m][p]
    fixed = fix(high_ref, low_ref, s_ref[...])
    for place in range(4):
        part = fixed[:, 128 * place : 128 * place + 128]
        w_ref[place] = part
        high, low = split(part)
        ws_ref[:, 256 * place : 256 * place + 128] = high
        ws_ref[:, 256 * place + 128 : 256 * place + 256] = low
    for place, half in enumerate((-2, -1, 0, 1)):
        steps = [d for d in REACH[half] if -1 <= half + d <= 2]
        picks, at = (pick_ref, OWN[half]) if half in OWN else (other_ref, OTHER[half])
        code, inv = known[half]
        total = neighbor_sum(ws_ref, half + steps[0] + 1, len(steps), picks, at + REACH[half].index(steps[0]), code)
        for m in range(2):
            weight = weight_ref[8 * m : 8 * m + 8, :] * inv
            for p in range(16):
                rows = slice(16 * p + 8 * m, 16 * p + 8 * m + 8)
                value = weight * total[m][p]
                if half >= -1:
                    value = value - w_ref[half + 1, rows, :]
                s_ref[rows, 128 * place : 128 * place + 128] = value
    fixed = fix(high_ref, low_ref, s_ref[...])
    for place, half in enumerate((-2, -1, 0, 1)):
        base = 4 * jnp.where(odd, 3 - place, place)
        for quad in range(4):
            parts = []
            for i in range(4):
                rows = slice(64 * quad + 16 * i, 64 * quad + 16 * i + 16)
                value = fixed[rows, 128 * place : 128 * place + 128]
                if half >= -1:
                    value = value + 2.0 * w_ref[half + 1, rows, :]
                if half >= 0:
                    value = value + u_ref[half, rows, :]
                parts.append(value)
            for j, part in enumerate(transpose_quads(parts)):
                out_ref[base + j, 16 * quad : 16 * quad + 16, :] = part


def to_levels_kernel(parts_ref, levels_ref, back_ref, out_ref, modes_ref):
    for group in range(8):
        for quad in range(4):
            rows = slice(16 * quad, 16 * quad + 16)
            modes_ref[16 * group : 16 * group + 16, 128 * quad : 128 * quad + 128] = (
                parts_ref[group, rows, :] + parts_ref[8 + group, rows, :]
            )
    high, low = split(dot3(levels_ref[...], modes_ref[...]))
    out_ref[...] = dot(high, back_ref[...]) + dot(low, back_ref[...])


def cost(flops, moved):
    return pl.CostEstimate(flops=flops, bytes_accessed=moved, transcendentals=0)


def near(x):
    return pltpu.with_memory_space_constraint(x, pltpu.VMEM)


def far(x):
    return pltpu.with_memory_space_constraint(x, pltpu.HBM)


VMEM = pl.BlockSpec(memory_space=pltpu.VMEM)
SMEM = pl.BlockSpec(memory_space=pltpu.SMEM)
HBM = pl.BlockSpec(memory_space=pltpu.HBM)
LIMIT = pltpu.CompilerParams(vmem_limit_bytes=20 << 20)


def body(blocks, levels_rhs, to_modes, from_modes, helmholtz, local_inverse, neighbor_ids, neighbor_count, orientation):
    axes = ("elem", "mode")
    parts = lax.axis_size("mode")
    source_pairs = [
        [((2 * k - 1 + i) % blocks) * parts + j for i in range(2) for j in range(parts)] for k in range(blocks // 2)
    ]
    target_pairs = [[(2 * k + i) * parts + j for i in range(2) for j in range(parts)] for k in range(blocks // 2)]
    source_swap = [(b, (((b + 1) ^ 1) - 1) % blocks) for b in range(blocks)]
    target_swap = [(b, b ^ 1) for b in range(blocks)]
    helmholtz = helmholtz[None]
    place = jnp.stack([(lax.axis_index("elem") + 1) % 2, lax.axis_index("mode")]).astype(jnp.int32)

    start, own = pl.pallas_call(
        to_modes_kernel,
        out_shape=(pltpu.VMEM((16, 64, 128), jnp.float32), pltpu.VMEM((24, 256), jnp.int32)),
        in_specs=[HBM] * 6,
        out_specs=(VMEM, VMEM),
        scratch_shapes=[
            pltpu.VMEM((128, 512), jnp.float32),
            pltpu.VMEM((128, 128), jnp.float32),
            pltpu.VMEM((1, 128), jnp.float32),
            pltpu.VMEM((1, 256), jnp.int32),
            pltpu.SemaphoreType.DMA((6,)),
        ],
        compiler_params=LIMIT,
        cost_estimate=cost(2 * 128 * 512 * (512 + 128), 1 << 20),
        name="to_modes_chunks",
    )(*[far(x) for x in (levels_rhs, to_modes, helmholtz, neighbor_ids, orientation, neighbor_count[None])])
    sources = lax.all_to_all(start, axes, 0, 0, axis_index_groups=source_pairs, tiled=True)
    source_table = lax.ppermute(own, "elem", source_swap)
    target_table = lax.ppermute(own, "elem", target_swap)
    *parts_of_tables, back = pl.pallas_call(
        tables_kernel,
        out_shape=(
            pltpu.VMEM((4, 6, 128, 256), jnp.bfloat16),
            pltpu.VMEM((2, 8, 128), jnp.int32),
            pltpu.VMEM((16, 128), jnp.float32),
            pltpu.VMEM((2, 8, 128), jnp.float32),
            pltpu.VMEM((256, 256), jnp.bfloat16),
            pltpu.VMEM((256, 256), jnp.bfloat16),
            pltpu.VMEM((512, 512), jnp.bfloat16),
        ),
        in_specs=[SMEM, VMEM, HBM, HBM],
        out_specs=(VMEM,) * 7,
        scratch_shapes=[
            pltpu.VMEM((1, 128), jnp.float32),
            pltpu.VMEM((16, 16), jnp.float32),
            pltpu.SemaphoreType.DMA((2,)),
        ],
        compiler_params=LIMIT,
        cost_estimate=cost(1 << 28, 2 << 20),
        name="own_tables",
    )(place, near(own), far(helmholtz), far(local_inverse))
    targets = pl.pallas_call(
        sweep_kernel,
        out_shape=pltpu.VMEM((16, 64, 128), jnp.float32),
        in_specs=[SMEM] + [VMEM] * 9,
        out_specs=VMEM,
        scratch_shapes=[
            pltpu.VMEM((4, 256, 128), jnp.float32),
            pltpu.VMEM((4, 256, 128), jnp.float32),
            pltpu.VMEM((256, 1024), jnp.bfloat16),
            pltpu.VMEM((256, 1024), jnp.bfloat16),
            pltpu.VMEM((256, 512), jnp.float32),
            pltpu.VMEM((4, 6, 128, 256), jnp.bfloat16),
        ],
        compiler_params=LIMIT,
        cost_estimate=cost(4 << 30, 8 << 20),
        name="two_sweeps",
    )(place, near(sources), near(target_table), near(source_table), *[near(part) for part in parts_of_tables])
    whole = lax.all_to_all(targets, axes, 0, 0, axis_index_groups=target_pairs, tiled=True)
    return pl.pallas_call(
        to_levels_kernel,
        out_shape=jax.ShapeDtypeStruct((128, 512), jnp.float32),
        in_specs=[VMEM] * 3,
        out_specs=VMEM,
        scratch_shapes=[pltpu.VMEM((128, 512), jnp.float32)],
        compiler_params=LIMIT,
        cost_estimate=cost(2 * 128 * 512 * (512 + 128), 1 << 20),
        name="to_levels",
    )(near(whole), from_modes, near(back))


def solution(mesh):
    in_specs = (
        P(None, ("elem", "mode")),
        P(),
        P(),
        P(),
        P(),
        P(None, "elem"),
        P("elem"),
        P(None, "elem"),
    )
    out_specs = P(None, ("elem", "mode"))
    return jax.shard_map(
        functools.partial(body, mesh.shape["elem"]), mesh=mesh, in_specs=in_specs, out_specs=out_specs, check_vma=False
    )
```

```python
import functools

import jax
import jax.numpy as jnp
from jax import lax
from jax.experimental import pallas as pl
from jax.experimental.pallas import tpu as pltpu
from jax.sharding import PartitionSpec as P


FIRST = 6


def spot(block, device):
    return 8 * block + (device - FIRST) % 8


def half_spot(odd, half, quarter):
    even_at, odd_at = (spot(at // 2, 4 * (at % 2) + quarter) for at in (half, 3 - half))
    return jnp.where(odd, odd_at, even_at)


def split(x):
    high = x.astype(jnp.bfloat16)
    return high, (x - high.astype(jnp.float32)).astype(jnp.bfloat16)


def dot(a, b):
    return jnp.dot(a, b, preferred_element_type=jnp.float32)


def dot3(a, b):
    ah, al = split(a)
    bh, bl = split(b)
    return dot(ah, bh) + (dot(ah, bl) + dot(al, bh))


def point_keys(index, spread):
    if spread:
        e, p = index >> 4, index & 15
        i, j = p >> 2, p & 3
        high_i, high_j = i >> 1, j >> 1
        a = jnp.where(high_i == 1, 3 - i, i)
        b = jnp.where(high_j == 1, 3 - j, j)
        return e * 4 + a * 2 + b, high_i * 2 + high_j
    t, e = index >> 5, index & 31
    return e * 4 + (t & 3), t >> 2


def parity_matrix(t, p, scale):
    i, j = p >> 2, p & 3
    near = jnp.where(i > 1, 3 - i, i) * 2 + jnp.where(j > 1, 3 - j, j)
    odd = ((i >> 1) * 2 + (j >> 1)) & (t >> 2)
    value = jnp.where((odd == 1) | (odd == 2), -scale, scale)
    return jnp.where(near == (t & 3), value, 0.0).astype(jnp.bfloat16)


def point_matrix(row_points, scale):
    row, row_bits = point_keys(lax.broadcasted_iota(jnp.int32, (512, 1), 0), row_points)
    col, col_bits = point_keys(lax.broadcasted_iota(jnp.int32, (1, 512), 1), not row_points)
    odd = row_bits & col_bits
    value = jnp.where((odd == 1) | (odd == 2), -scale, scale)
    return jnp.where(row == col, value, 0.0).astype(jnp.bfloat16)


def column(row):
    count = row.shape[1]
    at = lax.broadcasted_iota(jnp.int32, (count, count), 0) == lax.broadcasted_iota(jnp.int32, (count, count), 1)
    return jnp.sum(jnp.where(at, row, 0.0), axis=1, keepdims=True)


def fetch(pairs, sems):
    copies = [pltpu.make_async_copy(src, dst, sems.at[i]) for i, (src, dst) in enumerate(pairs)]
    for copy in copies:
        copy.start()
    return copies


def to_modes_kernel(
    rhs_hbm, modes_hbm, helmholtz_hbm, ids_hbm, orientation_hbm, count_hbm,
    out_ref, table_ref, rhs_ref, modes_ref, helmholtz_ref, count_ref, sems,
):
    copies = fetch(
        (
            (rhs_hbm, rhs_ref),
            (modes_hbm, modes_ref),
            (helmholtz_hbm, helmholtz_ref),
            (ids_hbm, table_ref.at[0:8]),
            (orientation_hbm, table_ref.at[8:16]),
            (count_hbm, count_ref),
        ),
        sems,
    )
    points = point_matrix(True, 1.0)
    for copy in copies:
        copy.wait()
    table_ref[16:24] = jnp.broadcast_to(count_ref[...], (8, 256))
    high, low = split(rhs_ref[...])
    high, low = split(dot(high, points) + dot(low, points))
    mh, ml = split(modes_ref[...] * column(1.0 / (1.0 + helmholtz_ref[...])))
    start = dot(mh, high) + (dot(mh, low) + dot(ml, high))
    for group in range(8):
        for quad in range(4):
            part = start[16 * group : 16 * group + 16, 128 * quad : 128 * quad + 128]
            for copy in range(2):
                out_ref[spot(copy, group), 16 * quad : 16 * quad + 16, :] = part


def transpose_quads(parts):
    rows = parts[0].shape[0]
    where_at = lax.broadcasted_iota(jnp.int32, (rows, 128), 1) // 32
    outs = []
    for i in range(4):
        out = None
        for j in range(4):
            shift = (32 * (j - i)) % 128
            moved = parts[j] if shift == 0 else pltpu.roll(parts[j], shift, 1)
            out = moved if out is None else jnp.where(where_at == j, moved, out)
        outs.append(out)
    return outs


REACH = {-2: (1,), -1: (0, 1), 0: (-1, 0, 1), 1: (-1, 0, 1), 2: (-1, 0, 1)}
OWN = {0: 0, 1: 3}
OTHER = {-2: 0, -1: 1, 2: 3}


def half_table(table_ref, half, odd):
    even_half, odd_half = half % 2, (half + 1) % 2
    even = table_ref[:, 128 * even_half : 128 * even_half + 128]
    other = table_ref[:, 128 * odd_half : 128 * odd_half + 128]
    step = jnp.where(odd, 1 + odd_half - (other[0:8] >> 7), (even[0:8] >> 7) - 1 - even_half)
    both = jnp.where(odd, other, even)
    count = both[16:24]
    slot = lax.broadcasted_iota(jnp.int32, (8, 128), 0)
    return both[0:8] & 127, jnp.where(slot < count, step, 9), both[8:16], 1.0 / count[0:1].astype(jnp.float32)


def write_picks(table_ref, half, odd, pick_ref, at):
    lane, step, code, inv = half_table(table_ref, half, odd)
    source = lax.broadcasted_iota(jnp.int32, (128, 128), 0)
    for i, d in enumerate(REACH[half]):
        wanted = jnp.where(step == d, lane, -1)
        for k in range(8):
            pick = (source == wanted[k : k + 1]).astype(jnp.float32).astype(jnp.bfloat16)
            pick_ref[k // 2, at + i, :, 128 * (k % 2) : 128 * (k % 2) + 128] = pick
    return code, inv


def tables_kernel(
    place_ref, own_ref, helmholtz_hbm, inverse_hbm,
    pick_ref, code_ref, weight_ref, inv_ref, high_ref, low_ref, back_ref, helmholtz_ref, inverse_ref, sems,
):
    copies = fetch(((helmholtz_hbm, helmholtz_ref), (inverse_hbm, inverse_ref)), sems)
    odd = place_ref[0] == 1
    for half in (0, 1):
        code, inv = write_picks(own_ref, half, odd, pick_ref, 3 * half)
        code_ref[half] = code
        inv_ref[half] = jnp.broadcast_to(inv, (8, 128))
    for copy in copies:
        copy.wait()
    back_ref[...] = point_matrix(False, 0.25)
    rows = lax.broadcasted_iota(jnp.int32, (16, 128), 0)
    lanes = lax.broadcasted_iota(jnp.int32, (16, 128), 1)
    coeff = jnp.sum(jnp.where(lanes == rows + 16 * place_ref[1], helmholtz_ref[...], 0.0), axis=1, keepdims=True)
    weight_ref[...] = jnp.broadcast_to(coeff / (1.0 + coeff), (16, 128))
    big = lax.broadcasted_iota(jnp.int32, (256, 16), 0) // 16 == lax.broadcasted_iota(jnp.int32, (256, 16), 1)
    rise = big.astype(jnp.float32).astype(jnp.bfloat16)
    wide = lax.broadcasted_iota(jnp.int32, (16, 256), 1) // 16 == lax.broadcasted_iota(jnp.int32, (16, 256), 0)
    spread = wide.astype(jnp.float32).astype(jnp.bfloat16)
    same = (
        lax.broadcasted_iota(jnp.int32, (256, 256), 0) % 16 == lax.broadcasted_iota(jnp.int32, (256, 256), 1) % 16
    )
    t = lax.broadcasted_iota(jnp.int32, (16, 16), 0)
    p = lax.broadcasted_iota(jnp.int32, (16, 16), 1)
    there = parity_matrix(t, p, 1.0)
    high, low = split(inverse_ref[...])
    high, low = split(dot(there, high) + dot(there, low))
    again = parity_matrix(p, t, 0.25)
    for ref, part in zip((high_ref, low_ref), split(dot(high, again) + dot(low, again))):
        ref[...] = jnp.where(same, dot(dot(rise, part).astype(jnp.bfloat16), spread), 0.0).astype(jnp.bfloat16)


def neighbor_sum(split_ref, first, count, pick_ref, at, code):
    total = [[None] * 16 for _ in range(2)]
    lhs = split_ref[:, 256 * first : 256 * (first + count)]
    for pair in range(4):
        rhs = jnp.concatenate([pick_ref[pair, at + c // 2] for c in range(2 * count)], axis=0)
        found = dot(lhs, rhs)
        for side in range(2):
            code_k = jnp.broadcast_to(code[2 * pair + side : 2 * pair + side + 1], (8, 128))
            swap = (code_k & 1) == 1
            by_row = jnp.where((code_k & 2) == 2, -1.0, 1.0)
            by_col = jnp.where((code_k & 4) == 4, -1.0, 1.0)
            by_both = by_row * by_col
            for m in range(2):
                x = [found[16 * p + 8 * m : 16 * p + 8 * m + 8, 128 * side : 128 * side + 128] for p in range(16)]
                even, col_odd, row_odd, odd = x[0:4], x[4:8], x[8:12], x[12:16]
                col_odd = [v * by_col for v in col_odd]
                row_odd = [v * by_row for v in row_odd]
                odd = [v * by_both for v in odd]
                turned = (0, 2, 1, 3)
                x = (
                    [even[i] if i == t else jnp.where(swap, even[t], even[i]) for i, t in enumerate(turned)]
                    + [jnp.where(swap, row_odd[t], col_odd[i]) for i, t in enumerate(turned)]
                    + [jnp.where(swap, col_odd[t], row_odd[i]) for i, t in enumerate(turned)]
                    + [odd[i] if i == t else jnp.where(swap, odd[t], odd[i]) for i, t in enumerate(turned)]
                )
                total[m] = [v if t is None else t + v for t, v in zip(total[m], x)]
    return total


def fix(high_ref, low_ref, x):
    xh, xl = split(x)
    return dot(high_ref[...], xh) + (dot(high_ref[...], xl) + dot(low_ref[...], xh))


def sweep_kernel(
    place_ref, x_ref, target_table_ref, source_table_ref, pick_ref, code_ref, weight_ref, inv_ref, high_ref, low_ref,
    out_ref, u_ref, w_ref, us_ref, ws_ref, s_ref, other_ref,
):
    odd = place_ref[0] == 1
    known = {half: (code_ref[half], inv_ref[half]) for half in OWN}
    for half in OTHER:
        table_ref = source_table_ref if half == 2 else target_table_ref
        known[half] = write_picks(table_ref, half, odd, other_ref, OTHER[half])
    for half in range(4):
        for quad in range(4):
            parts = [x_ref[half_spot(odd, half, j), 16 * quad : 16 * quad + 16, :] for j in range(4)]
            for i, part in enumerate(transpose_quads(parts)):
                rows = slice(64 * quad + 16 * i, 64 * quad + 16 * i + 16)
                u_ref[half, rows, :] = part
                high, low = split(part)
                us_ref[rows, 256 * half : 256 * half + 128] = high
                us_ref[rows, 256 * half + 128 : 256 * half + 256] = low
    for place, half in enumerate((-1, 0, 1, 2)):
        steps = [d for d in REACH[half] if 0 <= half + d <= 3]
        picks, at = (pick_ref, OWN[half]) if half in OWN else (other_ref, OTHER[half])
        code, inv = known[half]
        total = neighbor_sum(us_ref, half + steps[0], len(steps), picks, at + REACH[half].index(steps[0]), code)
        for m in range(2):
            weight = weight_ref[8 * m : 8 * m + 8, :] * inv
            for p in range(16):
                s_ref[16 * p + 8 * m : 16 * p + 8 * m + 8, 128 * place : 128 * place + 128] = weight * total[m][p]
    fixed = fix(high_ref, low_ref, s_ref[...])
    for place in range(4):
        part = fixed[:, 128 * place : 128 * place + 128]
        w_ref[place] = part
        high, low = split(part)
        ws_ref[:, 256 * place : 256 * place + 128] = high
        ws_ref[:, 256 * place + 128 : 256 * place + 256] = low
    for place, half in enumerate((-2, -1, 0, 1)):
        steps = [d for d in REACH[half] if -1 <= half + d <= 2]
        picks, at = (pick_ref, OWN[half]) if half in OWN else (other_ref, OTHER[half])
        code, inv = known[half]
        total = neighbor_sum(ws_ref, half + steps[0] + 1, len(steps), picks, at + REACH[half].index(steps[0]), code)
        for m in range(2):
            weight = weight_ref[8 * m : 8 * m + 8, :] * inv
            for p in range(16):
                rows = slice(16 * p + 8 * m, 16 * p + 8 * m + 8)
                value = weight * total[m][p]
                if half >= -1:
                    value = value - w_ref[half + 1, rows, :]
                s_ref[rows, 128 * place : 128 * place + 128] = value
    fixed = fix(high_ref, low_ref, s_ref[...])
    for place, half in enumerate((-2, -1, 0, 1)):
        for quad in range(4):
            parts = []
            for i in range(4):
                rows = slice(64 * quad + 16 * i, 64 * quad + 16 * i + 16)
                value = fixed[rows, 128 * place : 128 * place + 128]
                if half >= -1:
                    value = value + 2.0 * w_ref[half + 1, rows, :]
                if half >= 0:
                    value = value + u_ref[half, rows, :]
                parts.append(value)
            for j, part in enumerate(transpose_quads(parts)):
                out_ref[half_spot(odd, place, j), 16 * quad : 16 * quad + 16, :] = part


def to_levels_kernel(parts_ref, levels_ref, back_ref, out_ref, modes_ref):
    for group in range(8):
        for quad in range(4):
            rows = slice(16 * quad, 16 * quad + 16)
            modes_ref[16 * group : 16 * group + 16, 128 * quad : 128 * quad + 128] = (
                parts_ref[spot(0, group), rows, :] + parts_ref[spot(1, group), rows, :]
            )
    high, low = split(dot3(levels_ref[...], modes_ref[...]))
    out_ref[...] = dot(high, back_ref[...]) + dot(low, back_ref[...])


def cost(flops, moved):
    return pl.CostEstimate(flops=flops, bytes_accessed=moved, transcendentals=0)


def near(x):
    return pltpu.with_memory_space_constraint(x, pltpu.VMEM)


def far(x):
    return pltpu.with_memory_space_constraint(x, pltpu.HBM)


VMEM = pl.BlockSpec(memory_space=pltpu.VMEM)
SMEM = pl.BlockSpec(memory_space=pltpu.SMEM)
HBM = pl.BlockSpec(memory_space=pltpu.HBM)
LIMIT = pltpu.CompilerParams(vmem_limit_bytes=20 << 20)


def body(blocks, levels_rhs, to_modes, from_modes, helmholtz, local_inverse, neighbor_ids, neighbor_count, orientation):
    axes = ("elem", "mode")
    parts = lax.axis_size("mode")
    order = [(i, (j + FIRST) % parts) for i in range(2) for j in range(parts)]
    source_pairs = [[((2 * k - 1 + i) % blocks) * parts + j for i, j in order] for k in range(blocks // 2)]
    target_pairs = [[(2 * k + i) * parts + j for i, j in order] for k in range(blocks // 2)]
    source_swap = [(b, (((b + 1) ^ 1) - 1) % blocks) for b in range(blocks)]
    target_swap = [(b, b ^ 1) for b in range(blocks)]
    helmholtz = helmholtz[None]
    place = jnp.stack([(lax.axis_index("elem") + 1) % 2, lax.axis_index("mode")]).astype(jnp.int32)

    start, own = pl.pallas_call(
        to_modes_kernel,
        out_shape=(pltpu.VMEM((16, 64, 128), jnp.float32), pltpu.VMEM((24, 256), jnp.int32)),
        in_specs=[HBM] * 6,
        out_specs=(VMEM, VMEM),
        scratch_shapes=[
            pltpu.VMEM((128, 512), jnp.float32),
            pltpu.VMEM((128, 128), jnp.float32),
            pltpu.VMEM((1, 128), jnp.float32),
            pltpu.VMEM((1, 256), jnp.int32),
            pltpu.SemaphoreType.DMA((6,)),
        ],
        compiler_params=LIMIT,
        cost_estimate=cost(2 * 128 * 512 * (512 + 128), 1 << 20),
        name="to_modes_chunks",
    )(*[far(x) for x in (levels_rhs, to_modes, helmholtz, neighbor_ids, orientation, neighbor_count[None])])
    sources = lax.all_to_all(start, axes, 0, 0, axis_index_groups=source_pairs, tiled=True)
    source_table = lax.ppermute(own, "elem", source_swap)
    target_table = lax.ppermute(own, "elem", target_swap)
    *parts_of_tables, back = pl.pallas_call(
        tables_kernel,
        out_shape=(
            pltpu.VMEM((4, 6, 128, 256), jnp.bfloat16),
            pltpu.VMEM((2, 8, 128), jnp.int32),
            pltpu.VMEM((16, 128), jnp.float32),
            pltpu.VMEM((2, 8, 128), jnp.float32),
            pltpu.VMEM((256, 256), jnp.bfloat16),
            pltpu.VMEM((256, 256), jnp.bfloat16),
            pltpu.VMEM((512, 512), jnp.bfloat16),
        ),
        in_specs=[SMEM, VMEM, HBM, HBM],
        out_specs=(VMEM,) * 7,
        scratch_shapes=[
            pltpu.VMEM((1, 128), jnp.float32),
            pltpu.VMEM((16, 16), jnp.float32),
            pltpu.SemaphoreType.DMA((2,)),
        ],
        compiler_params=LIMIT,
        cost_estimate=cost(1 << 28, 2 << 20),
        name="own_tables",
    )(place, near(own), far(helmholtz), far(local_inverse))
    targets = pl.pallas_call(
        sweep_kernel,
        out_shape=pltpu.VMEM((16, 64, 128), jnp.float32),
        in_specs=[SMEM] + [VMEM] * 9,
        out_specs=VMEM,
        scratch_shapes=[
            pltpu.VMEM((4, 256, 128), jnp.float32),
            pltpu.VMEM((4, 256, 128), jnp.float32),
            pltpu.VMEM((256, 1024), jnp.bfloat16),
            pltpu.VMEM((256, 1024), jnp.bfloat16),
            pltpu.VMEM((256, 512), jnp.float32),
            pltpu.VMEM((4, 6, 128, 256), jnp.bfloat16),
        ],
        compiler_params=LIMIT,
        cost_estimate=cost(4 << 30, 8 << 20),
        name="two_sweeps",
    )(place, near(sources), near(target_table), near(source_table), *[near(part) for part in parts_of_tables])
    whole = lax.all_to_all(targets, axes, 0, 0, axis_index_groups=target_pairs, tiled=True)
    return pl.pallas_call(
        to_levels_kernel,
        out_shape=jax.ShapeDtypeStruct((128, 512), jnp.float32),
        in_specs=[VMEM] * 3,
        out_specs=VMEM,
        scratch_shapes=[pltpu.VMEM((128, 512), jnp.float32)],
        compiler_params=LIMIT,
        cost_estimate=cost(2 * 128 * 512 * (512 + 128), 1 << 20),
        name="to_levels",
    )(near(whole), from_modes, near(back))


def solution(mesh):
    in_specs = (
        P(None, ("elem", "mode")),
        P(),
        P(),
        P(),
        P(),
        P(None, "elem"),
        P("elem"),
        P(None, "elem"),
    )
    out_specs = P(None, ("elem", "mode"))
    return jax.shard_map(
        functools.partial(body, mesh.shape["elem"]), mesh=mesh, in_specs=in_specs, out_specs=out_specs, check_vma=False
    )
```

```python
import functools

import jax
import jax.numpy as jnp
from jax import lax
from jax.experimental import pallas as pl
from jax.experimental.pallas import tpu as pltpu
from jax.sharding import PartitionSpec as P


FIRST, SECOND = 6, 2


def spot(block, device, start):
    return 8 * block + (device - start) % 8


def half_spot(odd, half, quarter, start):
    even_at, odd_at = (spot(at // 2, 4 * (at % 2) + quarter, start) for at in (half, 3 - half))
    return jnp.where(odd, odd_at, even_at)


def split(x):
    high = x.astype(jnp.bfloat16)
    return high, (x - high.astype(jnp.float32)).astype(jnp.bfloat16)


def dot(a, b):
    return jnp.dot(a, b, preferred_element_type=jnp.float32)


def dot3(a, b):
    ah, al = split(a)
    bh, bl = split(b)
    return dot(ah, bh) + (dot(ah, bl) + dot(al, bh))


def point_keys(index, spread):
    if spread:
        e, p = index >> 4, index & 15
        i, j = p >> 2, p & 3
        high_i, high_j = i >> 1, j >> 1
        a = jnp.where(high_i == 1, 3 - i, i)
        b = jnp.where(high_j == 1, 3 - j, j)
        return e * 4 + a * 2 + b, high_i * 2 + high_j
    t, e = index >> 5, index & 31
    return e * 4 + (t & 3), t >> 2


def parity_matrix(t, p, scale):
    i, j = p >> 2, p & 3
    near = jnp.where(i > 1, 3 - i, i) * 2 + jnp.where(j > 1, 3 - j, j)
    odd = ((i >> 1) * 2 + (j >> 1)) & (t >> 2)
    value = jnp.where((odd == 1) | (odd == 2), -scale, scale)
    return jnp.where(near == (t & 3), value, 0.0).astype(jnp.bfloat16)


def point_matrix(row_points, scale):
    row, row_bits = point_keys(lax.broadcasted_iota(jnp.int32, (512, 1), 0), row_points)
    col, col_bits = point_keys(lax.broadcasted_iota(jnp.int32, (1, 512), 1), not row_points)
    odd = row_bits & col_bits
    value = jnp.where((odd == 1) | (odd == 2), -scale, scale)
    return jnp.where(row == col, value, 0.0).astype(jnp.bfloat16)


def column(row):
    count = row.shape[1]
    at = lax.broadcasted_iota(jnp.int32, (count, count), 0) == lax.broadcasted_iota(jnp.int32, (count, count), 1)
    return jnp.sum(jnp.where(at, row, 0.0), axis=1, keepdims=True)


def fetch(pairs, sems):
    copies = [pltpu.make_async_copy(src, dst, sems.at[i]) for i, (src, dst) in enumerate(pairs)]
    for copy in copies:
        copy.start()
    return copies


def to_modes_kernel(
    rhs_hbm, modes_hbm, helmholtz_hbm, ids_hbm, orientation_hbm, count_hbm,
    out_ref, table_ref, rhs_ref, modes_ref, helmholtz_ref, count_ref, sems,
):
    copies = fetch(
        (
            (rhs_hbm, rhs_ref),
            (modes_hbm, modes_ref),
            (helmholtz_hbm, helmholtz_ref),
            (ids_hbm, table_ref.at[0:8]),
            (orientation_hbm, table_ref.at[8:16]),
            (count_hbm, count_ref),
        ),
        sems,
    )
    points = point_matrix(True, 1.0)
    for copy in copies:
        copy.wait()
    table_ref[16:24] = jnp.broadcast_to(count_ref[...], (8, 256))
    high, low = split(rhs_ref[...])
    high, low = split(dot(high, points) + dot(low, points))
    mh, ml = split(modes_ref[...] * column(1.0 / (1.0 + helmholtz_ref[...])))
    start = dot(mh, high) + (dot(mh, low) + dot(ml, high))
    for group in range(8):
        for quad in range(4):
            part = start[16 * group : 16 * group + 16, 128 * quad : 128 * quad + 128]
            for copy in range(2):
                out_ref[spot(copy, group, FIRST), 16 * quad : 16 * quad + 16, :] = part


def transpose_quads(parts):
    rows = parts[0].shape[0]
    where_at = lax.broadcasted_iota(jnp.int32, (rows, 128), 1) // 32
    outs = []
    for i in range(4):
        out = None
        for j in range(4):
            shift = (32 * (j - i)) % 128
            moved = parts[j] if shift == 0 else pltpu.roll(parts[j], shift, 1)
            out = moved if out is None else jnp.where(where_at == j, moved, out)
        outs.append(out)
    return outs


REACH = {-2: (1,), -1: (0, 1), 0: (-1, 0, 1), 1: (-1, 0, 1), 2: (-1, 0, 1)}
OWN = {0: 0, 1: 3}
OTHER = {-2: 0, -1: 1, 2: 3}


def half_table(table_ref, half, odd):
    even_half, odd_half = half % 2, (half + 1) % 2
    even = table_ref[:, 128 * even_half : 128 * even_half + 128]
    other = table_ref[:, 128 * odd_half : 128 * odd_half + 128]
    step = jnp.where(odd, 1 + odd_half - (other[0:8] >> 7), (even[0:8] >> 7) - 1 - even_half)
    both = jnp.where(odd, other, even)
    count = both[16:24]
    slot = lax.broadcasted_iota(jnp.int32, (8, 128), 0)
    return both[0:8] & 127, jnp.where(slot < count, step, 9), both[8:16], 1.0 / count[0:1].astype(jnp.float32)


def write_picks(table_ref, half, odd, pick_ref, at):
    lane, step, code, inv = half_table(table_ref, half, odd)
    source = lax.broadcasted_iota(jnp.int32, (128, 128), 0)
    for i, d in enumerate(REACH[half]):
        wanted = jnp.where(step == d, lane, -1)
        for k in range(8):
            pick = (source == wanted[k : k + 1]).astype(jnp.float32).astype(jnp.bfloat16)
            pick_ref[k // 2, at + i, :, 128 * (k % 2) : 128 * (k % 2) + 128] = pick
    return code, inv


def tables_kernel(
    place_ref, own_ref, helmholtz_hbm, inverse_hbm,
    pick_ref, code_ref, weight_ref, inv_ref, high_ref, low_ref, back_ref, helmholtz_ref, inverse_ref, sems,
):
    copies = fetch(((helmholtz_hbm, helmholtz_ref), (inverse_hbm, inverse_ref)), sems)
    odd = place_ref[0] == 1
    for half in (0, 1):
        code, inv = write_picks(own_ref, half, odd, pick_ref, 3 * half)
        code_ref[half] = code
        inv_ref[half] = jnp.broadcast_to(inv, (8, 128))
    for copy in copies:
        copy.wait()
    back_ref[...] = point_matrix(False, 0.25)
    rows = lax.broadcasted_iota(jnp.int32, (16, 128), 0)
    lanes = lax.broadcasted_iota(jnp.int32, (16, 128), 1)
    coeff = jnp.sum(jnp.where(lanes == rows + 16 * place_ref[1], helmholtz_ref[...], 0.0), axis=1, keepdims=True)
    weight_ref[...] = jnp.broadcast_to(coeff / (1.0 + coeff), (16, 128))
    big = lax.broadcasted_iota(jnp.int32, (256, 16), 0) // 16 == lax.broadcasted_iota(jnp.int32, (256, 16), 1)
    rise = big.astype(jnp.float32).astype(jnp.bfloat16)
    wide = lax.broadcasted_iota(jnp.int32, (16, 256), 1) // 16 == lax.broadcasted_iota(jnp.int32, (16, 256), 0)
    spread = wide.astype(jnp.float32).astype(jnp.bfloat16)
    same = (
        lax.broadcasted_iota(jnp.int32, (256, 256), 0) % 16 == lax.broadcasted_iota(jnp.int32, (256, 256), 1) % 16
    )
    t = lax.broadcasted_iota(jnp.int32, (16, 16), 0)
    p = lax.broadcasted_iota(jnp.int32, (16, 16), 1)
    there = parity_matrix(t, p, 1.0)
    high, low = split(inverse_ref[...])
    high, low = split(dot(there, high) + dot(there, low))
    again = parity_matrix(p, t, 0.25)
    for ref, part in zip((high_ref, low_ref), split(dot(high, again) + dot(low, again))):
        ref[...] = jnp.where(same, dot(dot(rise, part).astype(jnp.bfloat16), spread), 0.0).astype(jnp.bfloat16)


def neighbor_sum(split_ref, first, count, pick_ref, at, code):
    total = [[None] * 16 for _ in range(2)]
    lhs = split_ref[:, 256 * first : 256 * (first + count)]
    for pair in range(4):
        rhs = jnp.concatenate([pick_ref[pair, at + c // 2] for c in range(2 * count)], axis=0)
        found = dot(lhs, rhs)
        for side in range(2):
            code_k = jnp.broadcast_to(code[2 * pair + side : 2 * pair + side + 1], (8, 128))
            swap = (code_k & 1) == 1
            by_row = jnp.where((code_k & 2) == 2, -1.0, 1.0)
            by_col = jnp.where((code_k & 4) == 4, -1.0, 1.0)
            by_both = by_row * by_col
            for m in range(2):
                x = [found[16 * p + 8 * m : 16 * p + 8 * m + 8, 128 * side : 128 * side + 128] for p in range(16)]
                even, col_odd, row_odd, odd = x[0:4], x[4:8], x[8:12], x[12:16]
                col_odd = [v * by_col for v in col_odd]
                row_odd = [v * by_row for v in row_odd]
                odd = [v * by_both for v in odd]
                turned = (0, 2, 1, 3)
                x = (
                    [even[i] if i == t else jnp.where(swap, even[t], even[i]) for i, t in enumerate(turned)]
                    + [jnp.where(swap, row_odd[t], col_odd[i]) for i, t in enumerate(turned)]
                    + [jnp.where(swap, col_odd[t], row_odd[i]) for i, t in enumerate(turned)]
                    + [odd[i] if i == t else jnp.where(swap, odd[t], odd[i]) for i, t in enumerate(turned)]
                )
                total[m] = [v if t is None else t + v for t, v in zip(total[m], x)]
    return total


def fix(high_ref, low_ref, x):
    xh, xl = split(x)
    return dot(high_ref[...], xh) + (dot(high_ref[...], xl) + dot(low_ref[...], xh))


def sweep_kernel(
    place_ref, x_ref, target_table_ref, source_table_ref, pick_ref, code_ref, weight_ref, inv_ref, high_ref, low_ref,
    out_ref, u_ref, w_ref, us_ref, ws_ref, s_ref, other_ref,
):
    odd = place_ref[0] == 1
    known = {half: (code_ref[half], inv_ref[half]) for half in OWN}
    for half in OTHER:
        table_ref = source_table_ref if half == 2 else target_table_ref
        known[half] = write_picks(table_ref, half, odd, other_ref, OTHER[half])
    for half in range(4):
        for quad in range(4):
            parts = [x_ref[half_spot(odd, half, j, FIRST), 16 * quad : 16 * quad + 16, :] for j in range(4)]
            for i, part in enumerate(transpose_quads(parts)):
                rows = slice(64 * quad + 16 * i, 64 * quad + 16 * i + 16)
                u_ref[half, rows, :] = part
                high, low = split(part)
                us_ref[rows, 256 * half : 256 * half + 128] = high
                us_ref[rows, 256 * half + 128 : 256 * half + 256] = low
    for place, half in enumerate((-1, 0, 1, 2)):
        steps = [d for d in REACH[half] if 0 <= half + d <= 3]
        picks, at = (pick_ref, OWN[half]) if half in OWN else (other_ref, OTHER[half])
        code, inv = known[half]
        total = neighbor_sum(us_ref, half + steps[0], len(steps), picks, at + REACH[half].index(steps[0]), code)
        for m in range(2):
            weight = weight_ref[8 * m : 8 * m + 8, :] * inv
            for p in range(16):
                s_ref[16 * p + 8 * m : 16 * p + 8 * m + 8, 128 * place : 128 * place + 128] = weight * total[m][p]
    fixed = fix(high_ref, low_ref, s_ref[...])
    for place in range(4):
        part = fixed[:, 128 * place : 128 * place + 128]
        w_ref[place] = part
        high, low = split(part)
        ws_ref[:, 256 * place : 256 * place + 128] = high
        ws_ref[:, 256 * place + 128 : 256 * place + 256] = low
    for place, half in enumerate((-2, -1, 0, 1)):
        steps = [d for d in REACH[half] if -1 <= half + d <= 2]
        picks, at = (pick_ref, OWN[half]) if half in OWN else (other_ref, OTHER[half])
        code, inv = known[half]
        total = neighbor_sum(ws_ref, half + steps[0] + 1, len(steps), picks, at + REACH[half].index(steps[0]), code)
        for m in range(2):
            weight = weight_ref[8 * m : 8 * m + 8, :] * inv
            for p in range(16):
                rows = slice(16 * p + 8 * m, 16 * p + 8 * m + 8)
                value = weight * total[m][p]
                if half >= -1:
                    value = value - w_ref[half + 1, rows, :]
                s_ref[rows, 128 * place : 128 * place + 128] = value
    fixed = fix(high_ref, low_ref, s_ref[...])
    for place, half in enumerate((-2, -1, 0, 1)):
        for quad in range(4):
            parts = []
            for i in range(4):
                rows = slice(64 * quad + 16 * i, 64 * quad + 16 * i + 16)
                value = fixed[rows, 128 * place : 128 * place + 128]
                if half >= -1:
                    value = value + 2.0 * w_ref[half + 1, rows, :]
                if half >= 0:
                    value = value + u_ref[half, rows, :]
                parts.append(value)
            for j, part in enumerate(transpose_quads(parts)):
                out_ref[half_spot(odd, place, j, SECOND), 16 * quad : 16 * quad + 16, :] = part


def to_levels_kernel(parts_ref, levels_ref, back_ref, out_ref, modes_ref):
    for group in range(8):
        for quad in range(4):
            rows = slice(16 * quad, 16 * quad + 16)
            modes_ref[16 * group : 16 * group + 16, 128 * quad : 128 * quad + 128] = (
                parts_ref[spot(0, group, SECOND), rows, :] + parts_ref[spot(1, group, SECOND), rows, :]
            )
    high, low = split(dot3(levels_ref[...], modes_ref[...]))
    out_ref[...] = dot(high, back_ref[...]) + dot(low, back_ref[...])


def cost(flops, moved):
    return pl.CostEstimate(flops=flops, bytes_accessed=moved, transcendentals=0)


def near(x):
    return pltpu.with_memory_space_constraint(x, pltpu.VMEM)


def far(x):
    return pltpu.with_memory_space_constraint(x, pltpu.HBM)


VMEM = pl.BlockSpec(memory_space=pltpu.VMEM)
SMEM = pl.BlockSpec(memory_space=pltpu.SMEM)
HBM = pl.BlockSpec(memory_space=pltpu.HBM)
LIMIT = pltpu.CompilerParams(vmem_limit_bytes=20 << 20)


def body(blocks, levels_rhs, to_modes, from_modes, helmholtz, local_inverse, neighbor_ids, neighbor_count, orientation):
    axes = ("elem", "mode")
    parts = lax.axis_size("mode")
    order = lambda start: [(i, (j + start) % parts) for i in range(2) for j in range(parts)]
    source_pairs = [[((2 * k - 1 + i) % blocks) * parts + j for i, j in order(FIRST)] for k in range(blocks // 2)]
    target_pairs = [[(2 * k + i) * parts + j for i, j in order(SECOND)] for k in range(blocks // 2)]
    source_swap = [(b, (((b + 1) ^ 1) - 1) % blocks) for b in range(blocks)]
    target_swap = [(b, b ^ 1) for b in range(blocks)]
    helmholtz = helmholtz[None]
    place = jnp.stack([(lax.axis_index("elem") + 1) % 2, lax.axis_index("mode")]).astype(jnp.int32)

    start, own = pl.pallas_call(
        to_modes_kernel,
        out_shape=(pltpu.VMEM((16, 64, 128), jnp.float32), pltpu.VMEM((24, 256), jnp.int32)),
        in_specs=[HBM] * 6,
        out_specs=(VMEM, VMEM),
        scratch_shapes=[
            pltpu.VMEM((128, 512), jnp.float32),
            pltpu.VMEM((128, 128), jnp.float32),
            pltpu.VMEM((1, 128), jnp.float32),
            pltpu.VMEM((1, 256), jnp.int32),
            pltpu.SemaphoreType.DMA((6,)),
        ],
        compiler_params=LIMIT,
        cost_estimate=cost(2 * 128 * 512 * (512 + 128), 1 << 20),
        name="to_modes_chunks",
    )(*[far(x) for x in (levels_rhs, to_modes, helmholtz, neighbor_ids, orientation, neighbor_count[None])])
    sources = lax.all_to_all(start, axes, 0, 0, axis_index_groups=source_pairs, tiled=True)
    source_table = lax.ppermute(own, "elem", source_swap)
    target_table = lax.ppermute(own, "elem", target_swap)
    *parts_of_tables, back = pl.pallas_call(
        tables_kernel,
        out_shape=(
            pltpu.VMEM((4, 6, 128, 256), jnp.bfloat16),
            pltpu.VMEM((2, 8, 128), jnp.int32),
            pltpu.VMEM((16, 128), jnp.float32),
            pltpu.VMEM((2, 8, 128), jnp.float32),
            pltpu.VMEM((256, 256), jnp.bfloat16),
            pltpu.VMEM((256, 256), jnp.bfloat16),
            pltpu.VMEM((512, 512), jnp.bfloat16),
        ),
        in_specs=[SMEM, VMEM, HBM, HBM],
        out_specs=(VMEM,) * 7,
        scratch_shapes=[
            pltpu.VMEM((1, 128), jnp.float32),
            pltpu.VMEM((16, 16), jnp.float32),
            pltpu.SemaphoreType.DMA((2,)),
        ],
        compiler_params=LIMIT,
        cost_estimate=cost(1 << 28, 2 << 20),
        name="own_tables",
    )(place, near(own), far(helmholtz), far(local_inverse))
    targets = pl.pallas_call(
        sweep_kernel,
        out_shape=pltpu.VMEM((16, 64, 128), jnp.float32),
        in_specs=[SMEM] + [VMEM] * 9,
        out_specs=VMEM,
        scratch_shapes=[
            pltpu.VMEM((4, 256, 128), jnp.float32),
            pltpu.VMEM((4, 256, 128), jnp.float32),
            pltpu.VMEM((256, 1024), jnp.bfloat16),
            pltpu.VMEM((256, 1024), jnp.bfloat16),
            pltpu.VMEM((256, 512), jnp.float32),
            pltpu.VMEM((4, 6, 128, 256), jnp.bfloat16),
        ],
        compiler_params=LIMIT,
        cost_estimate=cost(4 << 30, 8 << 20),
        name="two_sweeps",
    )(place, near(sources), near(target_table), near(source_table), *[near(part) for part in parts_of_tables])
    whole = lax.all_to_all(targets, axes, 0, 0, axis_index_groups=target_pairs, tiled=True)
    return pl.pallas_call(
        to_levels_kernel,
        out_shape=jax.ShapeDtypeStruct((128, 512), jnp.float32),
        in_specs=[VMEM] * 3,
        out_specs=VMEM,
        scratch_shapes=[pltpu.VMEM((128, 512), jnp.float32)],
        compiler_params=LIMIT,
        cost_estimate=cost(2 * 128 * 512 * (512 + 128), 1 << 20),
        name="to_levels",
    )(near(whole), from_modes, near(back))


def solution(mesh):
    in_specs = (
        P(None, ("elem", "mode")),
        P(),
        P(),
        P(),
        P(),
        P(None, "elem"),
        P("elem"),
        P(None, "elem"),
    )
    out_specs = P(None, ("elem", "mode"))
    return jax.shard_map(
        functools.partial(body, mesh.shape["elem"]), mesh=mesh, in_specs=in_specs, out_specs=out_specs, check_vma=False
    )
```
